128 devices in a mesh: rows: 64 (over y, z, x), cols: 2 (over core).
Axes of the slice: x: 4, y: 4, z: 4, core: 2. Of those that a mesh axis runs over, the one named last changes fastest.
Arguments:
- video: bfloat16 [512, 256, 256], P('rows', 'cols'), may hold values from -12 to 12
- foreground: float32 [512, 256, 256], P('rows', 'cols'), may hold values from -4 to 4
- scaled_dual: float32 [512, 256, 256], P('rows', 'cols'), may hold values from -2.5 to 2.5
Outputs:
- background: float32 [512, 256, 256], P('rows', 'cols')
- new_foreground: float32 [512, 256, 256], P('rows', 'cols')
- new_dual: float32 [512, 256, 256], P('rows', 'cols')
The draws below stay inside these ranges and needn't reach their ends.
All inputs are finite; a program needn't handle non-finite values.
Results may differ from the reference program's by a relative error of at most 0.00035.
Values sent between devices are 32-bit elements; how exact they have to be, the bound alone decides.
A program may use at most 64 MiB of HBM per device.

```python
import math
import jax
import jax.numpy as jnp
from jax import lax

F = 256
K_ROOT = 8
K_SIGN = 6
K_TV = 8
H = 512
W = 256


def draw_video(key, part):
    keys = jax.random.split(jax.random.fold_in(key, 7), 6)
    rank = 6
    spatial = jax.random.normal(keys[0], (H, W, rank), jnp.float32)
    weights = jnp.exp(jax.random.uniform(keys[2], (rank, 1), jnp.float32, -0.7, 0.7))
    temporal = jax.random.normal(keys[1], (rank, F), jnp.float32) * weights
    pattern = jnp.einsum('hwr,rf->hwf', spatial, temporal) / math.sqrt(rank)
    frame_scale = jnp.exp(jax.random.uniform(keys[3], (1, 1, F), jnp.float32, math.log(0.3), math.log(3.0)))
    pixel_scale = jnp.exp(jax.random.uniform(keys[5], (H, W, 1), jnp.float32, 0.0, math.log(3.0)))
    noise = jax.random.normal(keys[4], (H, W, F), jnp.float32)
    video = 1.2 * pattern + noise * frame_scale * pixel_scale
    return jnp.clip(video, -12.0, 12.0).astype(jnp.bfloat16)


def steps_of(own_key, dims, cuts, low, top_value):
    loudness = 1.0
    for position, parts in cuts:
        draws = jax.random.uniform(jax.random.fold_in(jax.random.fold_in(own_key, 6), position), (parts,), jnp.float32, low / len(cuts), top_value / len(cuts))
        loudness = loudness * jnp.repeat(jnp.exp(draws), dims[position] // parts).reshape((-1,) + (1,) * (len(dims) - 1 - position))
    return loudness


def centred(rng, shape, width, bound, cuts=(), kind=jnp.bfloat16):
    loudness = steps_of(rng, shape, cuts, -0.22, 0.18) if cuts else 1.0
    drawn = jax.random.normal(rng, shape, jnp.float32) * width * loudness
    return jnp.minimum(jnp.maximum(drawn, -bound), bound).astype(kind)


def setup_inputs(seed: int = 0) -> dict:
    key_of = jax.random.split(jax.random.key(seed), 4)
    return {
        "video": draw_video(jax.random.fold_in(key_of[3], 71), 0),
        "foreground": centred(key_of[1], (H, W, F), 0.5, 4.0, ((0, 64), (1, 2)), jnp.float32),
        "scaled_dual": centred(key_of[2], (H, W, F), 0.3, 2.5, ((0, 64), (1, 2)), jnp.float32),
    }


threshold_ratio = 1.0
dual_step = 0.25
tv_weight = 1.0

def matmul(left, right):
    return jnp.dot(left, right, precision=lax.Precision.HIGHEST, preferred_element_type=jnp.float32)

def shrink_matrix(gram):
    size = gram.shape[0]
    identity = jnp.eye(size, dtype=jnp.float32)
    scale = jnp.sqrt(jnp.sum(gram * gram))
    root = gram / scale
    inverse = identity
    for sweep in range(K_ROOT):
        factor = 1.5 * identity - 0.5 * matmul(inverse, root)
        root = matmul(root, factor)
        inverse = matmul(factor, inverse)
    cutoff = threshold_ratio * jnp.trace(root) / size
    signed = root - cutoff * identity
    for sweep in range(K_SIGN):
        signed = 1.5 * signed - 0.5 * matmul(signed, matmul(signed, signed))
    return 0.5 * matmul(identity - cutoff * inverse, identity + signed)

def divergence(dual_x, dual_y):
    prev_x = jnp.concatenate([jnp.zeros_like(dual_x[:1]), dual_x[:-1]], axis=0)
    prev_y = jnp.concatenate([jnp.zeros_like(dual_y[:, :1]), dual_y[:, :-1]], axis=1)
    return prev_x - dual_x + prev_y - dual_y

def slopes(frames):
    down = jnp.concatenate([frames[1:] - frames[:-1], jnp.zeros_like(frames[:1])], axis=0)
    across = jnp.concatenate([frames[:, 1:] - frames[:, :-1], jnp.zeros_like(frames[:, :1])], axis=1)
    return (down, across)

def reference(video, foreground, scaled_dual):
    frames = foreground.shape[2]
    observed = video.astype(jnp.float32)
    mixed = observed - foreground + scaled_dual
    flat = mixed.reshape(-1, frames)
    gram = matmul(flat.T, flat)
    shrink = shrink_matrix(gram)
    background = matmul(flat, shrink).reshape(foreground.shape)
    target = observed - background + scaled_dual
    dual_x = jnp.zeros_like(target)
    dual_y = jnp.zeros_like(target)
    for sweep in range(K_TV):
        current = target - divergence(dual_x, dual_y)
        down, across = slopes(current)
        dual_x = jnp.clip(dual_x + dual_step * down, -tv_weight, tv_weight)
        dual_y = jnp.clip(dual_y + dual_step * across, -tv_weight, tv_weight)
    new_foreground = target - divergence(dual_x, dual_y)
    new_dual = scaled_dual + observed - background - new_foreground
    return (background, new_foreground, new_dual)
```

```python
import jax
import jax.numpy as jnp
from jax import lax
from jax.sharding import PartitionSpec as P

K_ROOT = 8
K_SIGN = 6
K_TV = 8


threshold_ratio = 1.0
dual_step = 0.25
tv_weight = 1.0

HALO = K_TV


def shifted(x, axis, by):
    length = lax.axis_size(axis)
    pairs = [(i, i + by) for i in range(length) if 0 <= i + by < length]
    return lax.ppermute(x, axis, pairs)


def matmul(left, right):
    return jnp.dot(left, right, precision=lax.Precision.HIGHEST, preferred_element_type=jnp.float32)


def shrink_matrix(gram):
    size = gram.shape[0]
    identity = jnp.eye(size, dtype=jnp.float32)
    scale = jnp.sqrt(jnp.sum(gram * gram))
    root = gram / scale
    inverse = identity
    for sweep in range(K_ROOT):
        factor = 1.5 * identity - 0.5 * matmul(inverse, root)
        root = matmul(root, factor)
        inverse = matmul(factor, inverse)
    cutoff = threshold_ratio * jnp.trace(root) / size
    signed = root - cutoff * identity
    for sweep in range(K_SIGN):
        signed = 1.5 * signed - 0.5 * matmul(signed, matmul(signed, signed))
    return 0.5 * matmul(identity - cutoff * inverse, identity + signed)


def with_halo(pair):
    left = shifted(pair[:, :, -HALO:], "cols", 1)
    right = shifted(pair[:, :, :HALO], "cols", -1)
    pair = jnp.concatenate([left, pair, right], axis=2)
    up = shifted(pair[:, -HALO:], "rows", 1)
    down = shifted(pair[:, :HALO], "rows", -1)
    return jnp.concatenate([up, pair, down], axis=1)


def divergence(px, py):
    prev_x = jnp.concatenate([jnp.zeros_like(px[:1]), px[:-1]], axis=0)
    prev_y = jnp.concatenate([jnp.zeros_like(py[:, :1]), py[:, :-1]], axis=1)
    return prev_x - px + prev_y - py


def slopes(s):
    down = jnp.concatenate([s[1:] - s[:-1], jnp.zeros_like(s[:1])], axis=0)
    across = jnp.concatenate([s[:, 1:] - s[:, :-1], jnp.zeros_like(s[:, :1])], axis=1)
    return down, across


def per_device(video, foreground, scaled_dual):
    rows_here, cols_here, frames = foreground.shape
    total_rows = rows_here * lax.axis_size("rows")
    total_cols = cols_here * lax.axis_size("cols")
    observed = video.astype(jnp.float32)
    mixed = observed - foreground + scaled_dual
    a = observed + scaled_dual
    ext = with_halo(jnp.stack([a, mixed]))
    a_ext, mixed_ext = ext[0], ext[1]
    flat = mixed.reshape(-1, frames)
    gram = lax.psum(matmul(flat.T, flat), ("rows", "cols"))
    shrink = shrink_matrix(gram)
    ext_rows, ext_cols = rows_here + 2 * HALO, cols_here + 2 * HALO
    background_ext = matmul(mixed_ext.reshape(-1, frames), shrink).reshape(ext_rows, ext_cols, frames)
    target = a_ext - background_ext

    first_row = lax.axis_index("rows") * rows_here - HALO
    first_col = lax.axis_index("cols") * cols_here - HALO
    g = first_row + lax.broadcasted_iota(jnp.int32, (ext_rows, 1, 1), 0)
    h = first_col + lax.broadcasted_iota(jnp.int32, (1, ext_cols, 1), 1)
    keep_x = (g >= 0) & (g <= total_rows - 2)
    keep_y = (h >= 0) & (h <= total_cols - 2)

    dual_x = jnp.zeros_like(target)
    dual_y = jnp.zeros_like(target)
    for sweep in range(K_TV):
        current = target - divergence(dual_x, dual_y)
        down, across = slopes(current)
        dual_x = jnp.where(keep_x, jnp.clip(dual_x + dual_step * down, -tv_weight, tv_weight), 0.0)
        dual_y = jnp.where(keep_y, jnp.clip(dual_y + dual_step * across, -tv_weight, tv_weight), 0.0)
    inner = (slice(HALO, HALO + rows_here), slice(HALO, HALO + cols_here))
    new_foreground = (target - divergence(dual_x, dual_y))[inner]
    background = background_ext[inner]
    new_dual = target[inner] - new_foreground
    return (background, new_foreground, new_dual)


def solution(mesh):
    return jax.shard_map(
        per_device,
        mesh=mesh,
        in_specs=(P("rows", "cols", None), P("rows", "cols", None), P("rows", "cols", None)),
        out_specs=(P("rows", "cols", None), P("rows", "cols", None), P("rows", "cols", None)),
        check_vma=False,
    )
```

```python
import jax
import jax.numpy as jnp
from jax import lax
from jax.sharding import PartitionSpec as P

K_ROOT = 8
K_SIGN = 6
K_TV = 8


threshold_ratio = 1.0
dual_step = 0.25
tv_weight = 1.0

HALO = K_TV


def shifted(x, axis, by):
    length = lax.axis_size(axis)
    pairs = [(i, i + by) for i in range(length) if 0 <= i + by < length]
    return lax.ppermute(x, axis, pairs)


def matmul(left, right):
    return jnp.dot(left, right, precision=lax.Precision.HIGHEST, preferred_element_type=jnp.float32)


def shrink_matrix(gram):
    size = gram.shape[0]
    identity = jnp.eye(size, dtype=jnp.float32)
    scale = jnp.sqrt(jnp.sum(gram * gram))
    root = gram / scale
    inverse = identity
    for sweep in range(K_ROOT):
        factor = 1.5 * identity - 0.5 * matmul(inverse, root)
        root = matmul(root, factor)
        inverse = matmul(factor, inverse)
    cutoff = threshold_ratio * jnp.trace(root) / size
    signed = root - cutoff * identity
    for sweep in range(K_SIGN):
        signed = 1.5 * signed - 0.5 * matmul(signed, matmul(signed, signed))
    return 0.5 * matmul(identity - cutoff * inverse, identity + signed)


def with_halo(pair):
    up = shifted(pair[:, -HALO:], "rows", 1)
    down = shifted(pair[:, :HALO], "rows", -1)
    pair = jnp.concatenate([up, pair, down], axis=1)
    left = shifted(pair[:, :, -HALO:], "cols", 1)
    right = shifted(pair[:, :, :HALO], "cols", -1)
    return jnp.concatenate([left, pair, right], axis=2)


def all_sum(x):
    for axis in ("cols", "rows"):
        length = lax.axis_size(axis)
        if length & (length - 1):
            x = lax.psum(x, axis)
            continue
        step = 1
        while step < length:
            x = x + lax.ppermute(x, axis, [(i, i ^ step) for i in range(length)])
            step *= 2
    return x


def summed_gram(flat):
    local = matmul(flat.T, flat)
    half = local.shape[0] // 2
    packed = all_sum(jnp.concatenate([local[:half], local[half:, half:]], axis=1))
    top = packed[:, : 2 * half]
    corner = packed[:, 2 * half :]
    bottom = jnp.concatenate([top[:, half:].T, corner], axis=1)
    return jnp.concatenate([top, bottom], axis=0)


def divergence(px, py):
    prev_x = jnp.concatenate([jnp.zeros_like(px[:1]), px[:-1]], axis=0)
    prev_y = jnp.concatenate([jnp.zeros_like(py[:, :1]), py[:, :-1]], axis=1)
    return prev_x - px + prev_y - py


def slopes(s):
    down = jnp.concatenate([s[1:] - s[:-1], jnp.zeros_like(s[:1])], axis=0)
    across = jnp.concatenate([s[:, 1:] - s[:, :-1], jnp.zeros_like(s[:, :1])], axis=1)
    return down, across


def per_device(video, foreground, scaled_dual):
    rows_here, cols_here, frames = foreground.shape
    total_rows = rows_here * lax.axis_size("rows")
    total_cols = cols_here * lax.axis_size("cols")
    observed = video.astype(jnp.float32)
    mixed = observed - foreground + scaled_dual
    a = observed + scaled_dual
    ext = with_halo(jnp.stack([a, mixed]))
    a_ext, mixed_ext = ext[0], ext[1]
    flat = mixed.reshape(-1, frames)
    gram = summed_gram(flat)
    shrink = shrink_matrix(gram)
    ext_rows, ext_cols = rows_here + 2 * HALO, cols_here + 2 * HALO
    background_ext = matmul(mixed_ext.reshape(-1, frames), shrink).reshape(ext_rows, ext_cols, frames)
    target = a_ext - background_ext

    first_row = lax.axis_index("rows") * rows_here - HALO
    first_col = lax.axis_index("cols") * cols_here - HALO
    g = first_row + lax.broadcasted_iota(jnp.int32, (ext_rows, 1, 1), 0)
    h = first_col + lax.broadcasted_iota(jnp.int32, (1, ext_cols, 1), 1)
    keep_x = (g >= 0) & (g <= total_rows - 2)
    keep_y = (h >= 0) & (h <= total_cols - 2)

    dual_x = jnp.zeros_like(target)
    dual_y = jnp.zeros_like(target)
    for sweep in range(K_TV):
        current = target - divergence(dual_x, dual_y)
        down, across = slopes(current)
        dual_x = jnp.where(keep_x, jnp.clip(dual_x + dual_step * down, -tv_weight, tv_weight), 0.0)
        dual_y = jnp.where(keep_y, jnp.clip(dual_y + dual_step * across, -tv_weight, tv_weight), 0.0)
    inner = (slice(HALO, HALO + rows_here), slice(HALO, HALO + cols_here))
    new_foreground = (target - divergence(dual_x, dual_y))[inner]
    background = background_ext[inner]
    new_dual = target[inner] - new_foreground
    return (background, new_foreground, new_dual)


def solution(mesh):
    return jax.shard_map(
        per_device,
        mesh=mesh,
        in_specs=(P("rows", "cols", None), P("rows", "cols", None), P("rows", "cols", None)),
        out_specs=(P("rows", "cols", None), P("rows", "cols", None), P("rows", "cols", None)),
        check_vma=False,
    )
```

```python
import jax
import jax.numpy as jnp
from jax import lax
from jax.sharding import PartitionSpec as P
from jax.experimental import pallas as pl
from jax.experimental.pallas import tpu as pltpu

K_ROOT = 8
K_SIGN = 6
K_TV = 8


threshold_ratio = 1.0
dual_step = 0.25
tv_weight = 1.0

HALO = K_TV


def shifted(x, axis, by):
    length = lax.axis_size(axis)
    pairs = [(i, i + by) for i in range(length) if 0 <= i + by < length]
    return lax.ppermute(x, axis, pairs)


def matmul(left, right):
    return jnp.dot(left, right, precision=lax.Precision.HIGHEST, preferred_element_type=jnp.float32)


def shrink_matrix(gram):
    size = gram.shape[0]
    identity = jnp.eye(size, dtype=jnp.float32)
    scale = jnp.sqrt(jnp.sum(gram * gram))
    root = gram / scale
    inverse = identity
    for sweep in range(K_ROOT):
        factor = 1.5 * identity - 0.5 * matmul(inverse, root)
        root = matmul(root, factor)
        inverse = matmul(factor, inverse)
    cutoff = threshold_ratio * jnp.trace(root) / size
    signed = root - cutoff * identity
    for sweep in range(K_SIGN):
        signed = 1.5 * signed - 0.5 * matmul(signed, matmul(signed, signed))
    return 0.5 * matmul(identity - cutoff * inverse, identity + signed)


def with_halo(pair):
    up = shifted(pair[:, -HALO:], "rows", 1)
    down = shifted(pair[:, :HALO], "rows", -1)
    pair = jnp.concatenate([up, pair, down], axis=1)
    left = shifted(pair[:, :, -HALO:], "cols", 1)
    right = shifted(pair[:, :, :HALO], "cols", -1)
    return jnp.concatenate([left, pair, right], axis=2)


def all_sum(x):
    for axis in ("cols", "rows"):
        length = lax.axis_size(axis)
        if length & (length - 1):
            x = lax.psum(x, axis)
            continue
        step = 1
        while step < length:
            x = x + lax.ppermute(x, axis, [(i, i ^ step) for i in range(length)])
            step *= 2
    return x


def summed_gram(flat):
    local = matmul(flat.T, flat)
    half = local.shape[0] // 2
    packed = all_sum(jnp.concatenate([local[:half], local[half:, half:]], axis=1))
    top = packed[:, : 2 * half]
    corner = packed[:, 2 * half :]
    bottom = jnp.concatenate([top[:, half:].T, corner], axis=1)
    return jnp.concatenate([top, bottom], axis=0)


def divergence(px, py):
    prev_x = jnp.concatenate([jnp.zeros_like(px[:1]), px[:-1]], axis=0)
    prev_y = jnp.concatenate([jnp.zeros_like(py[:, :1]), py[:, :-1]], axis=1)
    return prev_x - px + prev_y - py


def slopes(s):
    down = jnp.concatenate([s[1:] - s[:-1], jnp.zeros_like(s[:1])], axis=0)
    across = jnp.concatenate([s[:, 1:] - s[:, :-1], jnp.zeros_like(s[:, :1])], axis=1)
    return down, across


def tv_kernel(target_ref, kx_ref, ky_ref, fg_ref, dual_ref):
    t = target_ref[...]
    rows, cols = t.shape[0], t.shape[1]
    kx = kx_ref[...]
    ky = ky_ref[...][None]

    def prev_y(q):
        return pltpu.roll(q, 1, 1)

    def next_y(q):
        return pltpu.roll(q, cols - 1, 1)

    s = t
    px = jnp.clip(dual_step * (s[1:] - s[:-1]), -tv_weight, tv_weight) * kx[: rows - 1]
    py = jnp.clip(dual_step * (next_y(s[: rows - 1]) - s[: rows - 1]), -tv_weight, tv_weight) * ky
    for sweep in range(2, K_TV + 1):
        n = rows + 3 - 2 * sweep
        q = py[1:n]
        s = t[sweep - 1 : rows + 1 - sweep] - (px[: n - 1] - px[1:n] + prev_y(q) - q)
        down = s[1:] - s[:-1]
        across = next_y(s[:-1]) - s[:-1]
        px = jnp.clip(px[1 : n - 1] + dual_step * down, -tv_weight, tv_weight) * kx[sweep - 1 : rows - sweep]
        py = jnp.clip(py[1 : n - 1] + dual_step * across, -tv_weight, tv_weight) * ky
    q = py[1:]
    inner = rows - 2 * HALO
    middle = t[HALO : HALO + inner]
    fg = middle - (px[:-1] - px[1:] + prev_y(q) - q)
    width = cols - 2 * HALO
    fg = fg[:, HALO : HALO + width]
    fg_ref[...] = fg
    dual_ref[...] = middle[:, HALO : HALO + width] - fg


def tv_local(target, kx, ky):
    rows, cols, frames = target.shape
    inner_rows, inner_cols = rows - 2 * HALO, cols - 2 * HALO
    lanes = 128 if frames % 128 == 0 else frames
    out = jax.ShapeDtypeStruct((inner_rows, inner_cols, frames), jnp.float32)
    return pl.pallas_call(
        tv_kernel,
        grid=(frames // lanes,),
        in_specs=[
            pl.BlockSpec((rows, cols, lanes), lambda f: (0, 0, f)),
            pl.BlockSpec((rows, 1, lanes), lambda f: (0, 0, 0)),
            pl.BlockSpec((cols, lanes), lambda f: (0, 0)),
        ],
        out_specs=[
            pl.BlockSpec((inner_rows, inner_cols, lanes), lambda f: (0, 0, f)),
            pl.BlockSpec((inner_rows, inner_cols, lanes), lambda f: (0, 0, f)),
        ],
        out_shape=[out, out],
    )(target, kx, ky)


def per_device(video, foreground, scaled_dual):
    rows_here, cols_here, frames = foreground.shape
    total_rows = rows_here * lax.axis_size("rows")
    total_cols = cols_here * lax.axis_size("cols")
    observed = video.astype(jnp.float32)
    mixed = observed - foreground + scaled_dual
    a = observed + scaled_dual
    ext = with_halo(jnp.stack([a, mixed]))
    a_ext, mixed_ext = ext[0], ext[1]
    flat = mixed.reshape(-1, frames)
    gram = summed_gram(flat)
    shrink = shrink_matrix(gram)
    ext_rows, ext_cols = rows_here + 2 * HALO, cols_here + 2 * HALO
    background_ext = matmul(mixed_ext.reshape(-1, frames), shrink).reshape(ext_rows, ext_cols, frames)
    target = a_ext - background_ext

    first_row = lax.axis_index("rows") * rows_here - HALO
    first_col = lax.axis_index("cols") * cols_here - HALO
    g = first_row + lax.broadcasted_iota(jnp.int32, (ext_rows, 1, 1), 0)
    h = first_col + lax.broadcasted_iota(jnp.int32, (1, ext_cols, 1), 1)
    keep_x = (g >= 0) & (g <= total_rows - 2)
    keep_y = (h >= 0) & (h <= total_cols - 2)
    lanes = 128 if frames % 128 == 0 else frames
    kx = jnp.broadcast_to(jnp.where(keep_x, 1.0, 0.0).astype(jnp.float32), (ext_rows, 1, lanes))
    ky = jnp.broadcast_to(jnp.where(keep_y, 1.0, 0.0).astype(jnp.float32)[0], (ext_cols, lanes))
    new_foreground, new_dual = tv_local(target, kx, ky)
    inner = (slice(HALO, HALO + rows_here), slice(HALO, HALO + cols_here))
    background = background_ext[inner]
    return (background, new_foreground, new_dual)


def solution(mesh):
    return jax.shard_map(
        per_device,
        mesh=mesh,
        in_specs=(P("rows", "cols", None), P("rows", "cols", None), P("rows", "cols", None)),
        out_specs=(P("rows", "cols", None), P("rows", "cols", None), P("rows", "cols", None)),
        check_vma=False,
    )
```

```python
import jax
import jax.numpy as jnp
from jax import lax
from jax.sharding import PartitionSpec as P
from jax.experimental import pallas as pl
from jax.experimental.pallas import tpu as pltpu


K_ROOT = 8
K_SIGN = 6
K_TV = 8


threshold_ratio = 1.0
dual_step = 0.25
tv_weight = 1.0

HALO = K_TV


def shifted(x, axis, by):
    length = lax.axis_size(axis)
    pairs = [(i, i + by) for i in range(length) if 0 <= i + by < length]
    return lax.ppermute(x, axis, pairs)


def matmul(left, right):
    return jnp.dot(left, right, precision=lax.Precision.HIGHEST, preferred_element_type=jnp.float32)


def shrink_matrix(gram):
    size = gram.shape[0]
    identity = jnp.eye(size, dtype=jnp.float32)
    scale = jnp.sqrt(jnp.sum(gram * gram))
    root = gram / scale
    inverse = identity
    for _ in range(K_ROOT):
        factor = 1.5 * identity - 0.5 * matmul(inverse, root)
        root = matmul(root, factor)
        inverse = matmul(factor, inverse)
    cutoff = threshold_ratio * jnp.trace(root) / size
    signed = root - cutoff * identity
    for _ in range(K_SIGN):
        signed = 1.5 * signed - 0.5 * matmul(signed, matmul(signed, signed))
    return 0.5 * matmul(identity - cutoff * inverse, identity + signed)


def with_halo(pair):
    up = shifted(pair[:, -HALO:], "rows", 1)
    down = shifted(pair[:, :HALO], "rows", -1)
    pair = jnp.concatenate([up, pair, down], axis=1)
    left = shifted(pair[:, :, -HALO:], "cols", 1)
    right = shifted(pair[:, :, :HALO], "cols", -1)
    return jnp.concatenate([left, pair, right], axis=2)


def all_sum(x):
    for axis in ("cols", "rows"):
        length = lax.axis_size(axis)
        if length & (length - 1):
            x = lax.psum(x, axis)
            continue
        step = 1
        while step < length:
            if 4 * step <= length:
                r1, r2, r3 = (lax.ppermute(x, axis, [(i, i ^ (k * step)) for i in range(length)]) for k in (1, 2, 3))
                x = (x + r1) + (r2 + r3)
                step *= 4
            else:
                x = x + lax.ppermute(x, axis, [(i, i ^ step) for i in range(length)])
                step *= 2
    return x


def summed_gram(flat):
    local = matmul(flat.T, flat)
    half = local.shape[0] // 2
    packed = all_sum(jnp.concatenate([local[:half], local[half:, half:]], axis=1))
    top = packed[:, : 2 * half]
    corner = packed[:, 2 * half :]
    bottom = jnp.concatenate([top[:, half:].T, corner], axis=1)
    return jnp.concatenate([top, bottom], axis=0)


def tv_kernel(target_ref, kx_ref, ky_ref, fg_ref, dual_ref):
    t = target_ref[...]
    rows, cols = t.shape[0], t.shape[1]
    kx = kx_ref[...]
    ky = ky_ref[...][None]

    def prev_y(q):
        return pltpu.roll(q, 1, 1)

    def next_y(q):
        return pltpu.roll(q, cols - 1, 1)

    s = t
    px = jnp.clip(dual_step * (s[1:] - s[:-1]), -tv_weight, tv_weight) * kx[: rows - 1]
    py = jnp.clip(dual_step * (next_y(s[: rows - 1]) - s[: rows - 1]), -tv_weight, tv_weight) * ky
    for sweep in range(2, K_TV + 1):
        n = rows + 3 - 2 * sweep
        q = py[1:n]
        s = t[sweep - 1 : rows + 1 - sweep] - (px[: n - 1] - px[1:n] + prev_y(q) - q)
        down = s[1:] - s[:-1]
        across = next_y(s[:-1]) - s[:-1]
        px = jnp.clip(px[1 : n - 1] + dual_step * down, -tv_weight, tv_weight) * kx[sweep - 1 : rows - sweep]
        py = jnp.clip(py[1 : n - 1] + dual_step * across, -tv_weight, tv_weight) * ky
    q = py[1:]
    inner = rows - 2 * HALO
    middle = t[HALO : HALO + inner]
    fg = middle - (px[:-1] - px[1:] + prev_y(q) - q)
    width = cols - 2 * HALO
    fg = fg[:, HALO : HALO + width]
    fg_ref[...] = fg
    dual_ref[...] = middle[:, HALO : HALO + width] - fg


def tv_local(target, kx, ky):
    rows, cols, frames = target.shape
    inner_rows, inner_cols = rows - 2 * HALO, cols - 2 * HALO
    lanes = 128 if frames % 128 == 0 else frames
    out = jax.ShapeDtypeStruct((inner_rows, inner_cols, frames), jnp.float32)
    return pl.pallas_call(
        tv_kernel,
        grid=(frames // lanes,),
        in_specs=[
            pl.BlockSpec((rows, cols, lanes), lambda f: (0, 0, f)),
            pl.BlockSpec((rows, 1, lanes), lambda f: (0, 0, 0)),
            pl.BlockSpec((cols, lanes), lambda f: (0, 0)),
        ],
        out_specs=[
            pl.BlockSpec((inner_rows, inner_cols, lanes), lambda f: (0, 0, f)),
            pl.BlockSpec((inner_rows, inner_cols, lanes), lambda f: (0, 0, f)),
        ],
        out_shape=[out, out],
    )(target, kx, ky)


def per_device(video, foreground, scaled_dual):
    rows_here, cols_here, frames = foreground.shape
    total_rows = rows_here * lax.axis_size("rows")
    total_cols = cols_here * lax.axis_size("cols")
    observed = video.astype(jnp.float32)
    mixed = observed - foreground + scaled_dual
    a = observed + scaled_dual
    ext = with_halo(jnp.stack([a, mixed]))
    a_ext, mixed_ext = ext[0], ext[1]
    flat = mixed.reshape(-1, frames)
    gram = summed_gram(flat)
    shrink = shrink_matrix(gram)
    ext_rows, ext_cols = rows_here + 2 * HALO, cols_here + 2 * HALO
    background_ext = matmul(mixed_ext.reshape(-1, frames), shrink).reshape(ext_rows, ext_cols, frames)
    target = a_ext - background_ext

    first_row = lax.axis_index("rows") * rows_here - HALO
    first_col = lax.axis_index("cols") * cols_here - HALO
    g = first_row + lax.broadcasted_iota(jnp.int32, (ext_rows, 1, 1), 0)
    h = first_col + lax.broadcasted_iota(jnp.int32, (1, ext_cols, 1), 1)
    keep_x = (g >= 0) & (g <= total_rows - 2)
    keep_y = (h >= 0) & (h <= total_cols - 2)
    lanes = 128 if frames % 128 == 0 else frames
    kx = jnp.broadcast_to(jnp.where(keep_x, 1.0, 0.0).astype(jnp.float32), (ext_rows, 1, lanes))
    ky = jnp.broadcast_to(jnp.where(keep_y, 1.0, 0.0).astype(jnp.float32)[0], (ext_cols, lanes))
    new_foreground, new_dual = tv_local(target, kx, ky)
    inner = (slice(HALO, HALO + rows_here), slice(HALO, HALO + cols_here))
    background = background_ext[inner]
    return (background, new_foreground, new_dual)


def solution(mesh):
    return jax.shard_map(
        per_device,
        mesh=mesh,
        in_specs=(P("rows", "cols", None), P("rows", "cols", None), P("rows", "cols", None)),
        out_specs=(P("rows", "cols", None), P("rows", "cols", None), P("rows", "cols", None)),
        check_vma=False,
    )
```

```python
import jax
import jax.numpy as jnp
from jax import lax
from jax.sharding import PartitionSpec as P
from jax.experimental import pallas as pl
from jax.experimental.pallas import tpu as pltpu


K_ROOT = 8
K_SIGN = 6
K_TV = 8


threshold_ratio = 1.0
dual_step = 0.25
tv_weight = 1.0

HALO = K_TV


def shifted(x, axis, by):
    length = lax.axis_size(axis)
    pairs = [(i, i + by) for i in range(length) if 0 <= i + by < length]
    return lax.ppermute(x, axis, pairs)


def matmul(left, right):
    return jnp.dot(left, right, precision=lax.Precision.HIGHEST, preferred_element_type=jnp.float32)


def shrink_matrix(gram):
    size = gram.shape[0]
    identity = jnp.eye(size, dtype=jnp.float32)
    scale = jnp.sqrt(jnp.sum(gram * gram))
    root = gram / scale
    inverse = identity
    for _ in range(K_ROOT):
        factor = 1.5 * identity - 0.5 * matmul(inverse, root)
        root = matmul(root, factor)
        inverse = matmul(factor, inverse)
    cutoff = threshold_ratio * jnp.trace(root) / size
    signed = root - cutoff * identity
    for _ in range(K_SIGN):
        signed = 1.5 * signed - 0.5 * matmul(signed, matmul(signed, signed))
    return 0.5 * matmul(identity - cutoff * inverse, identity + signed)


def with_halo(pair):
    up = shifted(pair[:, -HALO:], "rows", 1)
    down = shifted(pair[:, :HALO], "rows", -1)
    pair = jnp.concatenate([up, pair, down], axis=1)
    left = shifted(pair[:, :, -HALO:], "cols", 1)
    right = shifted(pair[:, :, :HALO], "cols", -1)
    return jnp.concatenate([left, pair, right], axis=2)


def all_sum(x):
    for axis in ("cols", "rows"):
        length = lax.axis_size(axis)
        if length & (length - 1):
            x = lax.psum(x, axis)
            continue
        groups, step = [], 1
        while step < length:
            radix = 4 if 4 * step <= length else 2
            groups.append((step, radix))
            step *= radix
        for step, radix in groups[1:] + groups[:1]:
            if radix == 4:
                r1, r2, r3 = (lax.ppermute(x, axis, [(i, i ^ (k * step)) for i in range(length)]) for k in (1, 2, 3))
                x = (x + r1) + (r2 + r3)
            else:
                x = x + lax.ppermute(x, axis, [(i, i ^ step) for i in range(length)])
    return x


def summed_gram(flat):
    local = matmul(flat.T, flat)
    half = local.shape[0] // 2
    packed = all_sum(jnp.concatenate([local[:half], local[half:, half:]], axis=1))
    top = packed[:, : 2 * half]
    corner = packed[:, 2 * half :]
    bottom = jnp.concatenate([top[:, half:].T, corner], axis=1)
    return jnp.concatenate([top, bottom], axis=0)


def tv_kernel(target_ref, kx_ref, ky_ref, fg_ref, dual_ref):
    t = target_ref[...]
    rows, cols = t.shape[0], t.shape[1]
    kx = kx_ref[...]
    ky = ky_ref[...][None]

    def prev_y(q):
        return pltpu.roll(q, 1, 1)

    def next_y(q):
        return pltpu.roll(q, cols - 1, 1)

    s = t
    px = jnp.clip(dual_step * (s[1:] - s[:-1]), -tv_weight, tv_weight) * kx[: rows - 1]
    py = jnp.clip(dual_step * (next_y(s[: rows - 1]) - s[: rows - 1]), -tv_weight, tv_weight) * ky
    for sweep in range(2, K_TV + 1):
        n = rows + 3 - 2 * sweep
        q = py[1:n]
        s = t[sweep - 1 : rows + 1 - sweep] - (px[: n - 1] - px[1:n] + prev_y(q) - q)
        down = s[1:] - s[:-1]
        across = next_y(s[:-1]) - s[:-1]
        px = jnp.clip(px[1 : n - 1] + dual_step * down, -tv_weight, tv_weight) * kx[sweep - 1 : rows - sweep]
        py = jnp.clip(py[1 : n - 1] + dual_step * across, -tv_weight, tv_weight) * ky
    q = py[1:]
    inner = rows - 2 * HALO
    middle = t[HALO : HALO + inner]
    fg = middle - (px[:-1] - px[1:] + prev_y(q) - q)
    width = cols - 2 * HALO
    fg = fg[:, HALO : HALO + width]
    fg_ref[...] = fg
    dual_ref[...] = middle[:, HALO : HALO + width] - fg


def tv_local(target, kx, ky):
    rows, cols, frames = target.shape
    inner_rows, inner_cols = rows - 2 * HALO, cols - 2 * HALO
    lanes = 128 if frames % 128 == 0 else frames
    out = jax.ShapeDtypeStruct((inner_rows, inner_cols, frames), jnp.float32)
    return pl.pallas_call(
        tv_kernel,
        grid=(frames // lanes,),
        in_specs=[
            pl.BlockSpec((rows, cols, lanes), lambda f: (0, 0, f)),
            pl.BlockSpec((rows, 1, lanes), lambda f: (0, 0, 0)),
            pl.BlockSpec((cols, lanes), lambda f: (0, 0)),
        ],
        out_specs=[
            pl.BlockSpec((inner_rows, inner_cols, lanes), lambda f: (0, 0, f)),
            pl.BlockSpec((inner_rows, inner_cols, lanes), lambda f: (0, 0, f)),
        ],
        out_shape=[out, out],
    )(target, kx, ky)


def per_device(video, foreground, scaled_dual):
    rows_here, cols_here, frames = foreground.shape
    total_rows = rows_here * lax.axis_size("rows")
    total_cols = cols_here * lax.axis_size("cols")
    observed = video.astype(jnp.float32)
    mixed = observed - foreground + scaled_dual
    a = observed + scaled_dual
    ext = with_halo(jnp.stack([a, mixed]))
    a_ext, mixed_ext = ext[0], ext[1]
    flat = mixed.reshape(-1, frames)
    gram = summed_gram(flat)
    shrink = shrink_matrix(gram)
    ext_rows, ext_cols = rows_here + 2 * HALO, cols_here + 2 * HALO
    background_ext = matmul(mixed_ext.reshape(-1, frames), shrink).reshape(ext_rows, ext_cols, frames)
    target = a_ext - background_ext

    first_row = lax.axis_index("rows") * rows_here - HALO
    first_col = lax.axis_index("cols") * cols_here - HALO
    g = first_row + lax.broadcasted_iota(jnp.int32, (ext_rows, 1, 1), 0)
    h = first_col + lax.broadcasted_iota(jnp.int32, (1, ext_cols, 1), 1)
    keep_x = (g >= 0) & (g <= total_rows - 2)
    keep_y = (h >= 0) & (h <= total_cols - 2)
    lanes = 128 if frames % 128 == 0 else frames
    kx = jnp.broadcast_to(jnp.where(keep_x, 1.0, 0.0).astype(jnp.float32), (ext_rows, 1, lanes))
    ky = jnp.broadcast_to(jnp.where(keep_y, 1.0, 0.0).astype(jnp.float32)[0], (ext_cols, lanes))
    new_foreground, new_dual = tv_local(target, kx, ky)
    inner = (slice(HALO, HALO + rows_here), slice(HALO, HALO + cols_here))
    background = background_ext[inner]
    return (background, new_foreground, new_dual)


def solution(mesh):
    return jax.shard_map(
        per_device,
        mesh=mesh,
        in_specs=(P("rows", "cols", None), P("rows", "cols", None), P("rows", "cols", None)),
        out_specs=(P("rows", "cols", None), P("rows", "cols", None), P("rows", "cols", None)),
        check_vma=False,
    )
```

```python
import jax
import jax.numpy as jnp
from jax import lax
from jax.sharding import PartitionSpec as P
from jax.experimental import pallas as pl
from jax.experimental.pallas import tpu as pltpu

K_ROOT = 8
K_SIGN = 6
K_TV = 8


threshold_ratio = 1.0
dual_step = 0.25
tv_weight = 1.0

HALO = K_TV


def shifted(x, axis, by):
    length = lax.axis_size(axis)
    pairs = [(i, i + by) for i in range(length) if 0 <= i + by < length]
    return lax.ppermute(x, axis, pairs)


def matmul(left, right):
    return jnp.dot(left, right, precision=lax.Precision.HIGHEST, preferred_element_type=jnp.float32)


def shrink_matrix(gram):
    size = gram.shape[0]
    identity = jnp.eye(size, dtype=jnp.float32)
    scale = jnp.sqrt(jnp.sum(gram * gram))
    root = gram / scale
    inverse = identity
    for _ in range(K_ROOT):
        factor = 1.5 * identity - 0.5 * matmul(inverse, root)
        root = matmul(root, factor)
        inverse = matmul(factor, inverse)
    cutoff = threshold_ratio * jnp.trace(root) / size
    signed = root - cutoff * identity
    for _ in range(K_SIGN):
        signed = 1.5 * signed - 0.5 * matmul(signed, matmul(signed, signed))
    return 0.5 * matmul(identity - cutoff * inverse, identity + signed)


def with_halo(pair):
    up = shifted(pair[:, -HALO:], "rows", 1)
    down = shifted(pair[:, :HALO], "rows", -1)
    pair = jnp.concatenate([up, pair, down], axis=1)
    left = shifted(pair[:, :, -HALO:], "cols", 1)
    right = shifted(pair[:, :, :HALO], "cols", -1)
    return jnp.concatenate([left, pair, right], axis=2)


def all_sum(x):
    for axis in ("cols", "rows"):
        length = lax.axis_size(axis)
        if length & (length - 1):
            x = lax.psum(x, axis)
            continue
        groups, step = [], 1
        while step < length:
            radix = 4 if 4 * step <= length else 2
            groups.append((step, radix))
            step *= radix
        for step, radix in groups:
            if radix == 4:
                r1, r2, r3 = (lax.ppermute(x, axis, [(i, i ^ (k * step)) for i in range(length)]) for k in (1, 2, 3))
                x = (x + r1) + (r2 + r3)
            else:
                x = x + lax.ppermute(x, axis, [(i, i ^ step) for i in range(length)])
    return x


def summed_gram(flat):
    local = matmul(flat.T, flat)
    half = local.shape[0] // 2
    packed = all_sum(jnp.concatenate([local[:half], local[half:, half:]], axis=1))
    top = packed[:, : 2 * half]
    corner = packed[:, 2 * half :]
    bottom = jnp.concatenate([top[:, half:].T, corner], axis=1)
    return jnp.concatenate([top, bottom], axis=0)


def tv_kernel(target_ref, kx_ref, ky_ref, fg_ref, dual_ref):
    t = target_ref[...]
    rows, cols = t.shape[0], t.shape[1]
    kx = kx_ref[...]
    ky = ky_ref[...][None]

    def prev_y(q):
        return pltpu.roll(q, 1, 1)

    def next_y(q):
        return pltpu.roll(q, cols - 1, 1)

    s = t
    px = jnp.clip(dual_step * (s[1:] - s[:-1]), -tv_weight, tv_weight) * kx[: rows - 1]
    py = jnp.clip(dual_step * (next_y(s[: rows - 1]) - s[: rows - 1]), -tv_weight, tv_weight) * ky
    for sweep in range(2, K_TV + 1):
        n = rows + 3 - 2 * sweep
        q = py[1:n]
        s = t[sweep - 1 : rows + 1 - sweep] - (px[: n - 1] - px[1:n] + prev_y(q) - q)
        down = s[1:] - s[:-1]
        across = next_y(s[:-1]) - s[:-1]
        px = jnp.clip(px[1 : n - 1] + dual_step * down, -tv_weight, tv_weight) * kx[sweep - 1 : rows - sweep]
        py = jnp.clip(py[1 : n - 1] + dual_step * across, -tv_weight, tv_weight) * ky
    q = py[1:]
    inner = rows - 2 * HALO
    middle = t[HALO : HALO + inner]
    fg = middle - (px[:-1] - px[1:] + prev_y(q) - q)
    width = cols - 2 * HALO
    fg = fg[:, HALO : HALO + width]
    fg_ref[...] = fg
    dual_ref[...] = middle[:, HALO : HALO + width] - fg


def tv_local(target, kx, ky):
    rows, cols, frames = target.shape
    inner_rows, inner_cols = rows - 2 * HALO, cols - 2 * HALO
    lanes = 128 if frames % 128 == 0 else frames
    out = jax.ShapeDtypeStruct((inner_rows, inner_cols, frames), jnp.float32)
    return pl.pallas_call(
        tv_kernel,
        grid=(frames // lanes,),
        in_specs=[
            pl.BlockSpec((rows, cols, lanes), lambda f: (0, 0, f)),
            pl.BlockSpec((rows, 1, lanes), lambda f: (0, 0, 0)),
            pl.BlockSpec((cols, lanes), lambda f: (0, 0)),
        ],
        out_specs=[
            pl.BlockSpec((inner_rows, inner_cols, lanes), lambda f: (0, 0, f)),
            pl.BlockSpec((inner_rows, inner_cols, lanes), lambda f: (0, 0, f)),
        ],
        out_shape=[out, out],
    )(target, kx, ky)


def per_device(video, foreground, scaled_dual):
    rows_here, cols_here, frames = foreground.shape
    total_rows = rows_here * lax.axis_size("rows")
    total_cols = cols_here * lax.axis_size("cols")
    observed = video.astype(jnp.float32)
    mixed = observed - foreground + scaled_dual
    flat = mixed.reshape(-1, frames)
    gram = summed_gram(flat)
    shrink = shrink_matrix(gram)
    background = matmul(flat, shrink).reshape(foreground.shape)
    target = observed - background + scaled_dual
    target = with_halo(target[None])[0]
    ext_rows, ext_cols = rows_here + 2 * HALO, cols_here + 2 * HALO

    first_row = lax.axis_index("rows") * rows_here - HALO
    first_col = lax.axis_index("cols") * cols_here - HALO
    g = first_row + lax.broadcasted_iota(jnp.int32, (ext_rows, 1, 1), 0)
    h = first_col + lax.broadcasted_iota(jnp.int32, (1, ext_cols, 1), 1)
    keep_x = (g >= 0) & (g <= total_rows - 2)
    keep_y = (h >= 0) & (h <= total_cols - 2)
    lanes = 128 if frames % 128 == 0 else frames
    kx = jnp.broadcast_to(jnp.where(keep_x, 1.0, 0.0).astype(jnp.float32), (ext_rows, 1, lanes))
    ky = jnp.broadcast_to(jnp.where(keep_y, 1.0, 0.0).astype(jnp.float32)[0], (ext_cols, lanes))
    new_foreground, new_dual = tv_local(target, kx, ky)
    return (background, new_foreground, new_dual)


def solution(mesh):
    return jax.shard_map(
        per_device,
        mesh=mesh,
        in_specs=(P("rows", "cols", None), P("rows", "cols", None), P("rows", "cols", None)),
        out_specs=(P("rows", "cols", None), P("rows", "cols", None), P("rows", "cols", None)),
        check_vma=False,
    )
```

```python
import jax
import jax.numpy as jnp
from jax import lax
from jax.sharding import PartitionSpec as P
from jax.experimental import pallas as pl
from jax.experimental.pallas import tpu as pltpu


K_ROOT = 8
K_SIGN = 6
K_TV = 8


threshold_ratio = 1.0
dual_step = 0.25
tv_weight = 1.0

HALO = K_TV


def shifted(x, axis, by):
    length = lax.axis_size(axis)
    pairs = [(i, i + by) for i in range(length) if 0 <= i + by < length]
    return lax.ppermute(x, axis, pairs)


def matmul(left, right):
    return jnp.dot(left, right, precision=lax.Precision.HIGHEST, preferred_element_type=jnp.float32)


def shrink_matrix(gram):
    size = gram.shape[0]
    identity = jnp.eye(size, dtype=jnp.float32)
    scale = jnp.sqrt(jnp.sum(gram * gram))
    root = gram / scale
    inverse = identity
    for _ in range(K_ROOT):
        factor = 1.5 * identity - 0.5 * matmul(inverse, root)
        root = matmul(root, factor)
        inverse = matmul(factor, inverse)
    cutoff = threshold_ratio * jnp.trace(root) / size
    signed = root - cutoff * identity
    for _ in range(K_SIGN):
        signed = 1.5 * signed - 0.5 * matmul(signed, matmul(signed, signed))
    return 0.5 * matmul(identity - cutoff * inverse, identity + signed)


def with_halo(pair):
    up = shifted(pair[:, -HALO:], "rows", 1)
    down = shifted(pair[:, :HALO], "rows", -1)
    pair = jnp.concatenate([up, pair, down], axis=1)
    left = shifted(pair[:, :, -HALO:], "cols", 1)
    right = shifted(pair[:, :, :HALO], "cols", -1)
    return jnp.concatenate([left, pair, right], axis=2)


def all_sum(x):
    for axis in ("cols", "rows"):
        length = lax.axis_size(axis)
        if length & (length - 1):
            x = lax.psum(x, axis)
            continue
        groups, step = [], 1
        while step < length:
            radix = 4 if 4 * step <= length else 2
            groups.append((step, radix))
            step *= radix
        for step, radix in groups:
            if radix == 4:
                r1, r2, r3 = (lax.ppermute(x, axis, [(i, i ^ (k * step)) for i in range(length)]) for k in (1, 2, 3))
                x = (x + r1) + (r2 + r3)
            else:
                x = x + lax.ppermute(x, axis, [(i, i ^ step) for i in range(length)])
    return x


def summed_gram(flat):
    local = matmul(flat.T, flat)
    half = local.shape[0] // 2
    packed = all_sum(jnp.concatenate([local[:half], local[half:, half:]], axis=1))
    top = packed[:, : 2 * half]
    corner = packed[:, 2 * half :]
    bottom = jnp.concatenate([top[:, half:].T, corner], axis=1)
    return jnp.concatenate([top, bottom], axis=0)


def tv_kernel(target_ref, kx_ref, ky_ref, fg_ref, dual_ref):
    t = target_ref[...]
    rows, cols = t.shape[0], t.shape[1]
    kx = kx_ref[...]
    ky = ky_ref[...][None]

    def prev_y(q):
        return pltpu.roll(q, 1, 1)

    def next_y(q):
        return pltpu.roll(q, cols - 1, 1)

    s = t
    px = jnp.clip(dual_step * (s[1:] - s[:-1]), -tv_weight, tv_weight) * kx[: rows - 1]
    py = jnp.clip(dual_step * (next_y(s[: rows - 1]) - s[: rows - 1]), -tv_weight, tv_weight) * ky
    for sweep in range(2, K_TV + 1):
        n = rows + 3 - 2 * sweep
        q = py[1:n]
        s = t[sweep - 1 : rows + 1 - sweep] - (px[: n - 1] - px[1:n] + prev_y(q) - q)
        down = s[1:] - s[:-1]
        across = next_y(s[:-1]) - s[:-1]
        px = jnp.clip(px[1 : n - 1] + dual_step * down, -tv_weight, tv_weight) * kx[sweep - 1 : rows - sweep]
        py = jnp.clip(py[1 : n - 1] + dual_step * across, -tv_weight, tv_weight) * ky
    q = py[1:]
    inner = rows - 2 * HALO
    middle = t[HALO : HALO + inner]
    fg = middle - (px[:-1] - px[1:] + prev_y(q) - q)
    width = cols - 2 * HALO
    fg = fg[:, HALO : HALO + width]
    fg_ref[...] = fg
    dual_ref[...] = middle[:, HALO : HALO + width] - fg


def tv_local(target, kx, ky, chunk, frames, into=None):
    rows, cols, lanes = target.shape
    inner_rows, inner_cols = rows - 2 * HALO, cols - 2 * HALO
    out = jax.ShapeDtypeStruct((inner_rows, inner_cols, frames), jnp.float32)
    in_specs = [
        pl.BlockSpec((rows, cols, lanes), lambda f: (0, 0, 0)),
        pl.BlockSpec((rows, 1, lanes), lambda f: (0, 0, 0)),
        pl.BlockSpec((cols, lanes), lambda f: (0, 0)),
    ]
    operands = [target, kx, ky]
    aliases = {}
    body = tv_kernel
    if into is not None:
        in_specs += [pl.BlockSpec(memory_space=pl.ANY), pl.BlockSpec(memory_space=pl.ANY)]
        operands += list(into)
        aliases = {3: 0, 4: 1}

        def body(target_ref, kx_ref, ky_ref, fg_in, dual_in, fg_ref, dual_ref):
            tv_kernel(target_ref, kx_ref, ky_ref, fg_ref, dual_ref)

    return pl.pallas_call(
        body,
        grid=(1,),
        in_specs=in_specs,
        out_specs=[
            pl.BlockSpec((inner_rows, inner_cols, lanes), lambda f: (0, 0, chunk)),
            pl.BlockSpec((inner_rows, inner_cols, lanes), lambda f: (0, 0, chunk)),
        ],
        out_shape=[out, out],
        input_output_aliases=aliases,
    )(*operands)


def per_device(video, foreground, scaled_dual):
    rows_here, cols_here, frames = foreground.shape
    total_rows = rows_here * lax.axis_size("rows")
    total_cols = cols_here * lax.axis_size("cols")
    observed = video.astype(jnp.float32)
    mixed = observed - foreground + scaled_dual
    flat = mixed.reshape(-1, frames)
    gram = summed_gram(flat)
    shrink = shrink_matrix(gram)
    background = matmul(flat, shrink).reshape(foreground.shape)
    target = observed - background + scaled_dual
    ext_rows, ext_cols = rows_here + 2 * HALO, cols_here + 2 * HALO

    first_row = lax.axis_index("rows") * rows_here - HALO
    first_col = lax.axis_index("cols") * cols_here - HALO
    g = first_row + lax.broadcasted_iota(jnp.int32, (ext_rows, 1, 1), 0)
    h = first_col + lax.broadcasted_iota(jnp.int32, (1, ext_cols, 1), 1)
    keep_x = (g >= 0) & (g <= total_rows - 2)
    keep_y = (h >= 0) & (h <= total_cols - 2)
    lanes = 128 if frames % 128 == 0 else frames
    kx = jnp.broadcast_to(jnp.where(keep_x, 1.0, 0.0).astype(jnp.float32), (ext_rows, 1, lanes))
    ky = jnp.broadcast_to(jnp.where(keep_y, 1.0, 0.0).astype(jnp.float32)[0], (ext_cols, lanes))
    outs = None
    for chunk in range(frames // lanes):
        piece = with_halo(target[None, :, :, chunk * lanes : (chunk + 1) * lanes])[0]
        outs = tv_local(piece, kx, ky, chunk, frames, outs)
    new_foreground, new_dual = outs
    return (background, new_foreground, new_dual)


def solution(mesh):
    return jax.shard_map(
        per_device,
        mesh=mesh,
        in_specs=(P("rows", "cols", None), P("rows", "cols", None), P("rows", "cols", None)),
        out_specs=(P("rows", "cols", None), P("rows", "cols", None), P("rows", "cols", None)),
        check_vma=False,
    )
```

```python
import jax
import jax.numpy as jnp
from jax import lax
from jax.sharding import PartitionSpec as P
from jax.experimental import pallas as pl
from jax.experimental.pallas import tpu as pltpu


K_ROOT = 8
K_SIGN = 6
K_TV = 8


threshold_ratio = 1.0
dual_step = 0.25
tv_weight = 1.0

HALO = K_TV


def shifted(x, axis, by):
    length = lax.axis_size(axis)
    pairs = [(i, i + by) for i in range(length) if 0 <= i + by < length]
    return lax.ppermute(x, axis, pairs)


def matmul(left, right):
    return jnp.dot(left, right, precision=lax.Precision.HIGHEST, preferred_element_type=jnp.float32)


def shrink_matrix(gram):
    size = gram.shape[0]
    identity = jnp.eye(size, dtype=jnp.float32)
    scale = jnp.sqrt(jnp.sum(gram * gram))
    root = gram / scale
    inverse = identity
    for _ in range(K_ROOT):
        factor = 1.5 * identity - 0.5 * matmul(inverse, root)
        root = matmul(root, factor)
        inverse = matmul(factor, inverse)
    cutoff = threshold_ratio * jnp.trace(root) / size
    signed = root - cutoff * identity
    for _ in range(K_SIGN):
        signed = 1.5 * signed - 0.5 * matmul(signed, matmul(signed, signed))
    return 0.5 * matmul(identity - cutoff * inverse, identity + signed)


def halo_pieces(block):
    left = shifted(block[:, -HALO:], "cols", 1)
    right = shifted(block[:, :HALO], "cols", -1)
    up = shifted(jnp.concatenate([left[-HALO:], block[-HALO:], right[-HALO:]], axis=1), "rows", 1)
    down = shifted(jnp.concatenate([left[:HALO], block[:HALO], right[:HALO]], axis=1), "rows", -1)
    return up, block, down, left, right


def all_sum(x):
    for axis in ("cols", "rows"):
        length = lax.axis_size(axis)
        if length & (length - 1):
            x = lax.psum(x, axis)
            continue
        groups, step = [], 1
        while step < length:
            radix = 4 if 4 * step <= length else 2
            groups.append((step, radix))
            step *= radix
        for step, radix in groups:
            if radix == 4:
                r1, r2, r3 = (lax.ppermute(x, axis, [(i, i ^ (k * step)) for i in range(length)]) for k in (1, 2, 3))
                x = (x + r1) + (r2 + r3)
            else:
                x = x + lax.ppermute(x, axis, [(i, i ^ step) for i in range(length)])
    return x


def summed_gram(flat):
    local = matmul(flat.T, flat)
    half = local.shape[0] // 2
    packed = all_sum(jnp.concatenate([local[:half], local[half:, half:]], axis=1))
    top = packed[:, : 2 * half]
    corner = packed[:, 2 * half :]
    bottom = jnp.concatenate([top[:, half:].T, corner], axis=1)
    return jnp.concatenate([top, bottom], axis=0)


def tv_kernel(up_ref, mid_ref, down_ref, left_ref, right_ref, kx_ref, ky_ref, fg_ref, dual_ref):
    t = jnp.concatenate([left_ref[...], mid_ref[...], right_ref[...]], axis=1)
    t = jnp.concatenate([up_ref[...], t, down_ref[...]], axis=0)
    rows, cols = t.shape[0], t.shape[1]
    kx = kx_ref[...]
    ky = ky_ref[...][None]

    def prev_y(q):
        return pltpu.roll(q, 1, 1)

    def next_y(q):
        return pltpu.roll(q, cols - 1, 1)

    s = t
    px = jnp.clip(dual_step * (s[1:] - s[:-1]), -tv_weight, tv_weight) * kx[: rows - 1]
    py = jnp.clip(dual_step * (next_y(s[: rows - 1]) - s[: rows - 1]), -tv_weight, tv_weight) * ky
    for sweep in range(2, K_TV + 1):
        n = rows + 3 - 2 * sweep
        q = py[1:n]
        s = t[sweep - 1 : rows + 1 - sweep] - (px[: n - 1] - px[1:n] + prev_y(q) - q)
        down = s[1:] - s[:-1]
        across = next_y(s[:-1]) - s[:-1]
        px = jnp.clip(px[1 : n - 1] + dual_step * down, -tv_weight, tv_weight) * kx[sweep - 1 : rows - sweep]
        py = jnp.clip(py[1 : n - 1] + dual_step * across, -tv_weight, tv_weight) * ky
    q = py[1:]
    inner = rows - 2 * HALO
    middle = t[HALO : HALO + inner]
    fg = middle - (px[:-1] - px[1:] + prev_y(q) - q)
    width = cols - 2 * HALO
    fg = fg[:, HALO : HALO + width]
    fg_ref[...] = fg
    dual_ref[...] = middle[:, HALO : HALO + width] - fg


def tv_local(pieces, kx, ky, chunk, frames, into=None):
    up, mid, down, left, right = pieces
    inner_rows, inner_cols, lanes = mid.shape
    rows, cols = inner_rows + 2 * HALO, inner_cols + 2 * HALO
    out = jax.ShapeDtypeStruct((inner_rows, inner_cols, frames), jnp.float32)

    def whole(shape):
        return pl.BlockSpec(shape, lambda f: (0,) * len(shape))

    in_specs = [whole(up.shape), whole(mid.shape), whole(down.shape), whole(left.shape), whole(right.shape)]
    in_specs += [whole((rows, 1, lanes)), whole((cols, lanes))]
    operands = [up, mid, down, left, right, kx, ky]
    aliases = {}
    body = tv_kernel
    if into is not None:
        in_specs += [pl.BlockSpec(memory_space=pl.ANY), pl.BlockSpec(memory_space=pl.ANY)]
        operands += list(into)
        aliases = {7: 0, 8: 1}

        def body(*refs):
            tv_kernel(*refs[:7], *refs[9:])

    return pl.pallas_call(
        body,
        grid=(1,),
        in_specs=in_specs,
        out_specs=[
            pl.BlockSpec((inner_rows, inner_cols, lanes), lambda f: (0, 0, chunk)),
            pl.BlockSpec((inner_rows, inner_cols, lanes), lambda f: (0, 0, chunk)),
        ],
        out_shape=[out, out],
        input_output_aliases=aliases,
    )(*operands)


def per_device(video, foreground, scaled_dual):
    rows_here, cols_here, frames = foreground.shape
    total_rows = rows_here * lax.axis_size("rows")
    total_cols = cols_here * lax.axis_size("cols")
    observed = video.astype(jnp.float32)
    mixed = observed - foreground + scaled_dual
    flat = mixed.reshape(-1, frames)
    gram = summed_gram(flat)
    shrink = shrink_matrix(gram)
    background = matmul(flat, shrink).reshape(foreground.shape)
    target = observed - background + scaled_dual
    ext_rows, ext_cols = rows_here + 2 * HALO, cols_here + 2 * HALO

    first_row = lax.axis_index("rows") * rows_here - HALO
    first_col = lax.axis_index("cols") * cols_here - HALO
    g = first_row + lax.broadcasted_iota(jnp.int32, (ext_rows, 1, 1), 0)
    h = first_col + lax.broadcasted_iota(jnp.int32, (1, ext_cols, 1), 1)
    lanes = 128 if frames % 128 == 0 else frames
    keep_x = (g >= 0) & (g <= total_rows - 2)
    keep_y = (h >= 0) & (h <= total_cols - 2)
    kx = jnp.broadcast_to(jnp.where(keep_x, 1.0, 0.0).astype(jnp.float32), (ext_rows, 1, lanes))
    ky = jnp.broadcast_to(jnp.where(keep_y, 1.0, 0.0).astype(jnp.float32)[0], (ext_cols, lanes))
    outs = None
    for chunk in range(frames // lanes):
        pieces = halo_pieces(target[:, :, chunk * lanes : (chunk + 1) * lanes])
        outs = tv_local(pieces, kx, ky, chunk, frames, outs)
    new_foreground, new_dual = outs
    return (background, new_foreground, new_dual)


def solution(mesh):
    return jax.shard_map(
        per_device,
        mesh=mesh,
        in_specs=(P("rows", "cols", None), P("rows", "cols", None), P("rows", "cols", None)),
        out_specs=(P("rows", "cols", None), P("rows", "cols", None), P("rows", "cols", None)),
        check_vma=False,
    )
```

```python
import jax
import jax.numpy as jnp
from jax import lax
from jax.sharding import PartitionSpec as P
from jax.experimental import pallas as pl
from jax.experimental.pallas import tpu as pltpu


K_ROOT = 8
K_SIGN = 6
K_TV = 8


threshold_ratio = 1.0
dual_step = 0.25
tv_weight = 1.0

HALO = K_TV


def shifted(x, axis, by):
    length = lax.axis_size(axis)
    pairs = [(i, i + by) for i in range(length) if 0 <= i + by < length]
    return lax.ppermute(x, axis, pairs)


def matmul(left, right):
    return jnp.dot(left, right, precision=lax.Precision.HIGHEST, preferred_element_type=jnp.float32)


def shrink_matrix(gram):
    size = gram.shape[0]
    identity = jnp.eye(size, dtype=jnp.float32)
    scale = jnp.sqrt(jnp.sum(gram * gram))
    root = gram / scale
    inverse = identity
    for _ in range(K_ROOT):
        factor = 1.5 * identity - 0.5 * matmul(inverse, root)
        both = matmul(jnp.concatenate([root, inverse], axis=0), factor)
        root, inverse = both[:size], both[size:]
    cutoff = threshold_ratio * jnp.trace(root) / size
    signed = root - cutoff * identity
    for _ in range(K_SIGN):
        signed = 1.5 * signed - 0.5 * matmul(signed, matmul(signed, signed))
    return 0.5 * matmul(identity - cutoff * inverse, identity + signed)


def halo_pieces(block):
    up = shifted(block[-HALO:], "rows", 1)
    down = shifted(block[:HALO], "rows", -1)
    left = shifted(jnp.concatenate([up[:, -HALO:], block[:, -HALO:], down[:, -HALO:]], axis=0), "cols", 1)
    right = shifted(jnp.concatenate([up[:, :HALO], block[:, :HALO], down[:, :HALO]], axis=0), "cols", -1)
    return up, block, down, left, right


def all_sum(x):
    for axis in ("cols", "rows"):
        length = lax.axis_size(axis)
        if length & (length - 1):
            x = lax.psum(x, axis)
            continue
        groups, step = [], 1
        while step < length:
            radix = 4 if 4 * step <= length else 2
            groups.append((step, radix))
            step *= radix
        for step, radix in groups:
            if radix == 4:
                r1, r2, r3 = (lax.ppermute(x, axis, [(i, i ^ (k * step)) for i in range(length)]) for k in (1, 2, 3))
                x = (x + r1) + (r2 + r3)
            else:
                x = x + lax.ppermute(x, axis, [(i, i ^ step) for i in range(length)])
    return x


def summed_gram(flat):
    local = matmul(flat.T, flat)
    half = local.shape[0] // 2
    packed = all_sum(jnp.concatenate([local[:half], local[half:, half:]], axis=1))
    top = packed[:, : 2 * half]
    corner = packed[:, 2 * half :]
    bottom = jnp.concatenate([top[:, half:].T, corner], axis=1)
    return jnp.concatenate([top, bottom], axis=0)


def tv_kernel(up_ref, mid_ref, down_ref, left_ref, right_ref, kx_ref, ky_ref, fg_ref, dual_ref):
    t = jnp.concatenate([up_ref[...], mid_ref[...], down_ref[...]], axis=0)
    t = jnp.concatenate([left_ref[...], t, right_ref[...]], axis=1)
    rows, cols = t.shape[0], t.shape[1]
    kx = kx_ref[...]
    ky = ky_ref[...][None]

    def prev_y(q):
        return pltpu.roll(q, 1, 1)

    def next_y(q):
        return pltpu.roll(q, cols - 1, 1)

    s = t
    px = jnp.clip(dual_step * (s[1:] - s[:-1]), -tv_weight, tv_weight) * kx[: rows - 1]
    py = jnp.clip(dual_step * (next_y(s[: rows - 1]) - s[: rows - 1]), -tv_weight, tv_weight) * ky
    for sweep in range(2, K_TV + 1):
        n = rows + 3 - 2 * sweep
        q = py[1:n]
        s = t[sweep - 1 : rows + 1 - sweep] - (px[: n - 1] - px[1:n] + prev_y(q) - q)
        down = s[1:] - s[:-1]
        across = next_y(s[:-1]) - s[:-1]
        px = jnp.clip(px[1 : n - 1] + dual_step * down, -tv_weight, tv_weight) * kx[sweep - 1 : rows - sweep]
        py = jnp.clip(py[1 : n - 1] + dual_step * across, -tv_weight, tv_weight) * ky
    q = py[1:]
    inner = rows - 2 * HALO
    middle = t[HALO : HALO + inner]
    fg = middle - (px[:-1] - px[1:] + prev_y(q) - q)
    width = cols - 2 * HALO
    fg = fg[:, HALO : HALO + width]
    fg_ref[...] = fg
    dual_ref[...] = middle[:, HALO : HALO + width] - fg


def tv_local(pieces, kx, ky, chunk, frames, into=None):
    up, mid, down, left, right = pieces
    inner_rows, inner_cols, lanes = mid.shape
    rows, cols = inner_rows + 2 * HALO, inner_cols + 2 * HALO
    out = jax.ShapeDtypeStruct((inner_rows, inner_cols, frames), jnp.float32)

    def whole(shape):
        return pl.BlockSpec(shape, lambda f: (0,) * len(shape))

    in_specs = [whole(up.shape), whole(mid.shape), whole(down.shape), whole(left.shape), whole(right.shape)]
    in_specs += [whole((rows, 1, lanes)), whole((cols, lanes))]
    operands = [up, mid, down, left, right, kx, ky]
    aliases = {}
    body = tv_kernel
    if into is not None:
        in_specs += [pl.BlockSpec(memory_space=pl.ANY), pl.BlockSpec(memory_space=pl.ANY)]
        operands += list(into)
        aliases = {7: 0, 8: 1}

        def body(*refs):
            tv_kernel(*refs[:7], *refs[9:])

    return pl.pallas_call(
        body,
        grid=(1,),
        in_specs=in_specs,
        out_specs=[
            pl.BlockSpec((inner_rows, inner_cols, lanes), lambda f: (0, 0, chunk)),
            pl.BlockSpec((inner_rows, inner_cols, lanes), lambda f: (0, 0, chunk)),
        ],
        out_shape=[out, out],
        input_output_aliases=aliases,
    )(*operands)


def per_device(video, foreground, scaled_dual):
    rows_here, cols_here, frames = foreground.shape
    total_rows = rows_here * lax.axis_size("rows")
    total_cols = cols_here * lax.axis_size("cols")
    observed = video.astype(jnp.float32)
    mixed = observed - foreground + scaled_dual
    flat = mixed.reshape(-1, frames)
    gram = summed_gram(flat)
    shrink = shrink_matrix(gram)
    background = matmul(flat, shrink).reshape(foreground.shape)
    target = observed - background + scaled_dual
    ext_rows, ext_cols = rows_here + 2 * HALO, cols_here + 2 * HALO

    first_row = lax.axis_index("rows") * rows_here - HALO
    first_col = lax.axis_index("cols") * cols_here - HALO
    g = first_row + lax.broadcasted_iota(jnp.int32, (ext_rows, 1, 1), 0)
    h = first_col + lax.broadcasted_iota(jnp.int32, (1, ext_cols, 1), 1)
    lanes = 128 if frames % 128 == 0 else frames
    keep_x = (g >= 0) & (g <= total_rows - 2)
    keep_y = (h >= 0) & (h <= total_cols - 2)
    kx = jnp.broadcast_to(jnp.where(keep_x, 1.0, 0.0).astype(jnp.float32), (ext_rows, 1, lanes))
    ky = jnp.broadcast_to(jnp.where(keep_y, 1.0, 0.0).astype(jnp.float32)[0], (ext_cols, lanes))
    outs = None
    for chunk in range(frames // lanes):
        pieces = halo_pieces(target[:, :, chunk * lanes : (chunk + 1) * lanes])
        outs = tv_local(pieces, kx, ky, chunk, frames, outs)
    new_foreground, new_dual = outs
    return (background, new_foreground, new_dual)


def solution(mesh):
    return jax.shard_map(
        per_device,
        mesh=mesh,
        in_specs=(P("rows", "cols", None), P("rows", "cols", None), P("rows", "cols", None)),
        out_specs=(P("rows", "cols", None), P("rows", "cols", None), P("rows", "cols", None)),
        check_vma=False,
    )
```

```python
import jax
import jax.numpy as jnp
from jax import lax
from jax.sharding import PartitionSpec as P
from jax.experimental import pallas as pl
from jax.experimental.pallas import tpu as pltpu


K_ROOT = 8
K_SIGN = 6
K_TV = 8


threshold_ratio = 1.0
dual_step = 0.25
tv_weight = 1.0

HALO = K_TV


def shifted(x, axis, by):
    length = lax.axis_size(axis)
    pairs = [(i, i + by) for i in range(length) if 0 <= i + by < length]
    return lax.ppermute(x, axis, pairs)


def matmul(left, right):
    return jnp.dot(left, right, precision=lax.Precision.HIGHEST, preferred_element_type=jnp.float32)


def shrink_kernel(gram_ref, out_ref):
    gram = gram_ref[...]
    size = gram.shape[0]
    identity = (lax.broadcasted_iota(jnp.int32, gram.shape, 0) == lax.broadcasted_iota(jnp.int32, gram.shape, 1)).astype(jnp.float32)
    scale = jnp.sqrt(jnp.sum(gram * gram, keepdims=True))
    root = gram / scale
    inverse = identity
    for _ in range(K_ROOT):
        factor = 1.5 * identity - 0.5 * matmul(inverse, root)
        root = matmul(root, factor)
        inverse = matmul(factor, inverse)
    cutoff = threshold_ratio * jnp.sum(root * identity, keepdims=True) / size
    signed = root - cutoff * identity
    for _ in range(K_SIGN):
        signed = 1.5 * signed - 0.5 * matmul(signed, matmul(signed, signed))
    out_ref[...] = 0.5 * matmul(identity - cutoff * inverse, identity + signed)


def shrink_in_vmem(gram):
    return pl.pallas_call(shrink_kernel, out_shape=jax.ShapeDtypeStruct(gram.shape, jnp.float32))(gram)


def halo_pieces(block):
    up = shifted(block[-HALO:], "rows", 1)
    down = shifted(block[:HALO], "rows", -1)
    left = shifted(jnp.concatenate([up[:, -HALO:], block[:, -HALO:], down[:, -HALO:]], axis=0), "cols", 1)
    right = shifted(jnp.concatenate([up[:, :HALO], block[:, :HALO], down[:, :HALO]], axis=0), "cols", -1)
    return up, block, down, left, right


def all_sum(x):
    for axis in ("cols", "rows"):
        length = lax.axis_size(axis)
        if length & (length - 1):
            x = lax.psum(x, axis)
            continue
        groups, step = [], 1
        while step < length:
            radix = 4 if 4 * step <= length else 2
            groups.append((step, radix))
            step *= radix
        for step, radix in groups:
            if radix == 4:
                r1, r2, r3 = (lax.ppermute(x, axis, [(i, i ^ (k * step)) for i in range(length)]) for k in (1, 2, 3))
                x = (x + r1) + (r2 + r3)
            else:
                x = x + lax.ppermute(x, axis, [(i, i ^ step) for i in range(length)])
    return x


def summed_gram(flat):
    local = matmul(flat.T, flat)
    half = local.shape[0] // 2
    packed = all_sum(jnp.concatenate([local[:half], local[half:, half:]], axis=1))
    top = packed[:, : 2 * half]
    corner = packed[:, 2 * half :]
    bottom = jnp.concatenate([top[:, half:].T, corner], axis=1)
    return jnp.concatenate([top, bottom], axis=0)


def tv_kernel(up_ref, mid_ref, down_ref, left_ref, right_ref, kx_ref, ky_ref, fg_ref, dual_ref):
    t = jnp.concatenate([up_ref[...], mid_ref[...], down_ref[...]], axis=0)
    t = jnp.concatenate([left_ref[...], t, right_ref[...]], axis=1)
    rows, cols = t.shape[0], t.shape[1]
    kx = kx_ref[...]
    ky = ky_ref[...][None]

    def prev_y(q):
        return pltpu.roll(q, 1, 1)

    def next_y(q):
        return pltpu.roll(q, cols - 1, 1)

    s = t
    px = jnp.clip(dual_step * (s[1:] - s[:-1]), -tv_weight, tv_weight) * kx[: rows - 1]
    py = jnp.clip(dual_step * (next_y(s[: rows - 1]) - s[: rows - 1]), -tv_weight, tv_weight) * ky
    for sweep in range(2, K_TV + 1):
        n = rows + 3 - 2 * sweep
        q = py[1:n]
        s = t[sweep - 1 : rows + 1 - sweep] - (px[: n - 1] - px[1:n] + prev_y(q) - q)
        down = s[1:] - s[:-1]
        across = next_y(s[:-1]) - s[:-1]
        px = jnp.clip(px[1 : n - 1] + dual_step * down, -tv_weight, tv_weight) * kx[sweep - 1 : rows - sweep]
        py = jnp.clip(py[1 : n - 1] + dual_step * across, -tv_weight, tv_weight) * ky
    q = py[1:]
    inner = rows - 2 * HALO
    middle = t[HALO : HALO + inner]
    fg = middle - (px[:-1] - px[1:] + prev_y(q) - q)
    width = cols - 2 * HALO
    fg = fg[:, HALO : HALO + width]
    fg_ref[...] = fg
    dual_ref[...] = middle[:, HALO : HALO + width] - fg


def tv_local(pieces, kx, ky, chunk, frames, into=None):
    up, mid, down, left, right = pieces
    inner_rows, inner_cols, lanes = mid.shape
    rows, cols = inner_rows + 2 * HALO, inner_cols + 2 * HALO
    out = jax.ShapeDtypeStruct((inner_rows, inner_cols, frames), jnp.float32)

    def whole(shape):
        return pl.BlockSpec(shape, lambda f: (0,) * len(shape))

    in_specs = [whole(up.shape), whole(mid.shape), whole(down.shape), whole(left.shape), whole(right.shape)]
    in_specs += [whole((rows, 1, lanes)), whole((cols, lanes))]
    operands = [up, mid, down, left, right, kx, ky]
    aliases = {}
    body = tv_kernel
    if into is not None:
        in_specs += [pl.BlockSpec(memory_space=pl.ANY), pl.BlockSpec(memory_space=pl.ANY)]
        operands += list(into)
        aliases = {7: 0, 8: 1}

        def body(*refs):
            tv_kernel(*refs[:7], *refs[9:])

    return pl.pallas_call(
        body,
        grid=(1,),
        in_specs=in_specs,
        out_specs=[
            pl.BlockSpec((inner_rows, inner_cols, lanes), lambda f: (0, 0, chunk)),
            pl.BlockSpec((inner_rows, inner_cols, lanes), lambda f: (0, 0, chunk)),
        ],
        out_shape=[out, out],
        input_output_aliases=aliases,
    )(*operands)


def per_device(video, foreground, scaled_dual):
    rows_here, cols_here, frames = foreground.shape
    total_rows = rows_here * lax.axis_size("rows")
    total_cols = cols_here * lax.axis_size("cols")
    observed = video.astype(jnp.float32)
    mixed = observed - foreground + scaled_dual
    flat = mixed.reshape(-1, frames)
    gram = summed_gram(flat)
    shrink = shrink_in_vmem(gram)
    background = matmul(flat, shrink).reshape(foreground.shape)
    target = observed - background + scaled_dual
    ext_rows, ext_cols = rows_here + 2 * HALO, cols_here + 2 * HALO

    first_row = lax.axis_index("rows") * rows_here - HALO
    first_col = lax.axis_index("cols") * cols_here - HALO
    g = first_row + lax.broadcasted_iota(jnp.int32, (ext_rows, 1, 1), 0)
    h = first_col + lax.broadcasted_iota(jnp.int32, (1, ext_cols, 1), 1)
    lanes = 128 if frames % 128 == 0 else frames
    keep_x = (g >= 0) & (g <= total_rows - 2)
    keep_y = (h >= 0) & (h <= total_cols - 2)
    kx = jnp.broadcast_to(jnp.where(keep_x, 1.0, 0.0).astype(jnp.float32), (ext_rows, 1, lanes))
    ky = jnp.broadcast_to(jnp.where(keep_y, 1.0, 0.0).astype(jnp.float32)[0], (ext_cols, lanes))
    outs = None
    for chunk in range(frames // lanes):
        pieces = halo_pieces(target[:, :, chunk * lanes : (chunk + 1) * lanes])
        outs = tv_local(pieces, kx, ky, chunk, frames, outs)
    new_foreground, new_dual = outs
    return (background, new_foreground, new_dual)


def solution(mesh):
    return jax.shard_map(
        per_device,
        mesh=mesh,
        in_specs=(P("rows", "cols", None), P("rows", "cols", None), P("rows", "cols", None)),
        out_specs=(P("rows", "cols", None), P("rows", "cols", None), P("rows", "cols", None)),
        check_vma=False,
    )
```

```python
import jax
import jax.numpy as jnp
from jax import lax
from jax.sharding import PartitionSpec as P
from jax.experimental import pallas as pl
from jax.experimental.pallas import tpu as pltpu


K_ROOT = 8
K_SIGN = 6
K_TV = 8


threshold_ratio = 1.0
dual_step = 0.25
tv_weight = 1.0

HALO = K_TV


def shifted(x, axis, by):
    length = lax.axis_size(axis)
    pairs = [(i, i + by) for i in range(length) if 0 <= i + by < length]
    return lax.ppermute(x, axis, pairs)


def matmul(left, right):
    return jnp.dot(left, right, precision=lax.Precision.HIGH, preferred_element_type=jnp.float32)


def shrink_matrix(gram):
    size = gram.shape[0]
    identity = jnp.eye(size, dtype=jnp.float32)
    scale = jnp.sqrt(jnp.sum(gram * gram))
    root = gram / scale
    inverse = identity
    for _ in range(K_ROOT):
        factor = 1.5 * identity - 0.5 * matmul(inverse, root)
        root = matmul(root, factor)
        inverse = matmul(factor, inverse)
    cutoff = threshold_ratio * jnp.trace(root) / size
    signed = root - cutoff * identity
    for _ in range(K_SIGN):
        signed = 1.5 * signed - 0.5 * matmul(signed, matmul(signed, signed))
    return 0.5 * matmul(identity - cutoff * inverse, identity + signed)


def halo_pieces(block):
    up = shifted(block[-HALO:], "rows", 1)
    down = shifted(block[:HALO], "rows", -1)
    left = shifted(jnp.concatenate([up[:, -HALO:], block[:, -HALO:], down[:, -HALO:]], axis=0), "cols", 1)
    right = shifted(jnp.concatenate([up[:, :HALO], block[:, :HALO], down[:, :HALO]], axis=0), "cols", -1)
    return up, block, down, left, right


def all_sum(x):
    for axis in ("cols", "rows"):
        length = lax.axis_size(axis)
        if length & (length - 1):
            x = lax.psum(x, axis)
            continue
        groups, step = [], 1
        while step < length:
            radix = 4 if 4 * step <= length else 2
            groups.append((step, radix))
            step *= radix
        for step, radix in groups:
            if radix == 4:
                r1, r2, r3 = (lax.ppermute(x, axis, [(i, i ^ (k * step)) for i in range(length)]) for k in (1, 2, 3))
                x = (x + r1) + (r2 + r3)
            else:
                x = x + lax.ppermute(x, axis, [(i, i ^ step) for i in range(length)])
    return x


def summed_gram(flat):
    local = matmul(flat.T, flat)
    half = local.shape[0] // 2
    packed = all_sum(jnp.concatenate([local[:half], local[half:, half:]], axis=1))
    top = packed[:, : 2 * half]
    corner = packed[:, 2 * half :]
    bottom = jnp.concatenate([top[:, half:].T, corner], axis=1)
    return jnp.concatenate([top, bottom], axis=0)


def tv_kernel(up_ref, mid_ref, down_ref, left_ref, right_ref, kx_ref, ky_ref, fg_ref, dual_ref):
    t = jnp.concatenate([up_ref[...], mid_ref[...], down_ref[...]], axis=0)
    t = jnp.concatenate([left_ref[...], t, right_ref[...]], axis=1)
    rows, cols = t.shape[0], t.shape[1]
    kx = kx_ref[...]
    ky = ky_ref[...][None]

    def prev_y(q):
        return pltpu.roll(q, 1, 1)

    def next_y(q):
        return pltpu.roll(q, cols - 1, 1)

    s = t
    px = jnp.clip(dual_step * (s[1:] - s[:-1]), -tv_weight, tv_weight) * kx[: rows - 1]
    py = jnp.clip(dual_step * (next_y(s[: rows - 1]) - s[: rows - 1]), -tv_weight, tv_weight) * ky
    for sweep in range(2, K_TV + 1):
        n = rows + 3 - 2 * sweep
        q = py[1:n]
        s = t[sweep - 1 : rows + 1 - sweep] - (px[: n - 1] - px[1:n] + prev_y(q) - q)
        down = s[1:] - s[:-1]
        across = next_y(s[:-1]) - s[:-1]
        px = jnp.clip(px[1 : n - 1] + dual_step * down, -tv_weight, tv_weight) * kx[sweep - 1 : rows - sweep]
        py = jnp.clip(py[1 : n - 1] + dual_step * across, -tv_weight, tv_weight) * ky
    q = py[1:]
    inner = rows - 2 * HALO
    middle = t[HALO : HALO + inner]
    fg = middle - (px[:-1] - px[1:] + prev_y(q) - q)
    width = cols - 2 * HALO
    fg = fg[:, HALO : HALO + width]
    fg_ref[...] = fg
    dual_ref[...] = middle[:, HALO : HALO + width] - fg


def tv_local(pieces, kx, ky, chunk, frames, into=None):
    up, mid, down, left, right = pieces
    inner_rows, inner_cols, lanes = mid.shape
    rows, cols = inner_rows + 2 * HALO, inner_cols + 2 * HALO
    out = jax.ShapeDtypeStruct((inner_rows, inner_cols, frames), jnp.float32)

    def whole(shape):
        return pl.BlockSpec(shape, lambda f: (0,) * len(shape))

    in_specs = [whole(up.shape), whole(mid.shape), whole(down.shape), whole(left.shape), whole(right.shape)]
    in_specs += [whole((rows, 1, lanes)), whole((cols, lanes))]
    operands = [up, mid, down, left, right, kx, ky]
    aliases = {}
    body = tv_kernel
    if into is not None:
        in_specs += [pl.BlockSpec(memory_space=pl.ANY), pl.BlockSpec(memory_space=pl.ANY)]
        operands += list(into)
        aliases = {7: 0, 8: 1}

        def body(*refs):
            tv_kernel(*refs[:7], *refs[9:])

    return pl.pallas_call(
        body,
        grid=(1,),
        in_specs=in_specs,
        out_specs=[
            pl.BlockSpec((inner_rows, inner_cols, lanes), lambda f: (0, 0, chunk)),
            pl.BlockSpec((inner_rows, inner_cols, lanes), lambda f: (0, 0, chunk)),
        ],
        out_shape=[out, out],
        input_output_aliases=aliases,
    )(*operands)


def per_device(video, foreground, scaled_dual):
    rows_here, cols_here, frames = foreground.shape
    total_rows = rows_here * lax.axis_size("rows")
    total_cols = cols_here * lax.axis_size("cols")
    observed = video.astype(jnp.float32)
    mixed = observed - foreground + scaled_dual
    flat = mixed.reshape(-1, frames)
    gram = summed_gram(flat)
    shrink = shrink_matrix(gram)
    background = matmul(flat, shrink).reshape(foreground.shape)
    target = observed - background + scaled_dual
    ext_rows, ext_cols = rows_here + 2 * HALO, cols_here + 2 * HALO

    first_row = lax.axis_index("rows") * rows_here - HALO
    first_col = lax.axis_index("cols") * cols_here - HALO
    g = first_row + lax.broadcasted_iota(jnp.int32, (ext_rows, 1, 1), 0)
    h = first_col + lax.broadcasted_iota(jnp.int32, (1, ext_cols, 1), 1)
    lanes = 128 if frames % 128 == 0 else frames
    keep_x = (g >= 0) & (g <= total_rows - 2)
    keep_y = (h >= 0) & (h <= total_cols - 2)
    kx = jnp.broadcast_to(jnp.where(keep_x, 1.0, 0.0).astype(jnp.float32), (ext_rows, 1, lanes))
    ky = jnp.broadcast_to(jnp.where(keep_y, 1.0, 0.0).astype(jnp.float32)[0], (ext_cols, lanes))
    outs = None
    for chunk in range(frames // lanes):
        pieces = halo_pieces(target[:, :, chunk * lanes : (chunk + 1) * lanes])
        outs = tv_local(pieces, kx, ky, chunk, frames, outs)
    new_foreground, new_dual = outs
    return (background, new_foreground, new_dual)


def solution(mesh):
    return jax.shard_map(
        per_device,
        mesh=mesh,
        in_specs=(P("rows", "cols", None), P("rows", "cols", None), P("rows", "cols", None)),
        out_specs=(P("rows", "cols", None), P("rows", "cols", None), P("rows", "cols", None)),
        check_vma=False,
    )
```

```python
import jax
import jax.numpy as jnp
from jax import lax
from jax.sharding import PartitionSpec as P
from jax.experimental import pallas as pl
from jax.experimental.pallas import tpu as pltpu


K_ROOT = 8
K_SIGN = 6
K_TV = 8


threshold_ratio = 1.0
dual_step = 0.25
tv_weight = 1.0

HALO = K_TV


def shifted(x, axis, by):
    length = lax.axis_size(axis)
    pairs = [(i, i + by) for i in range(length) if 0 <= i + by < length]
    return lax.ppermute(x, axis, pairs)


def matmul(left, right):
    return jnp.dot(left, right, precision=lax.Precision.HIGH, preferred_element_type=jnp.float32)


def shrink_matrix(gram):
    size = gram.shape[0]
    identity = jnp.eye(size, dtype=jnp.float32)
    scale = jnp.sqrt(jnp.sum(gram * gram))
    root = gram / scale
    inverse = identity
    for _ in range(K_ROOT):
        factor = 1.5 * identity - 0.5 * matmul(inverse, root)
        root = matmul(root, factor)
        inverse = matmul(factor, inverse)
    cutoff = threshold_ratio * jnp.trace(root) / size
    signed = root - cutoff * identity
    for _ in range(K_SIGN):
        signed = 1.5 * signed - 0.5 * matmul(signed, matmul(signed, signed))
    return 0.5 * matmul(identity - cutoff * inverse, identity + signed)


def halo_pieces(block, cols_first=False):
    if cols_first:
        left = shifted(block[:, -HALO:], "cols", 1)
        right = shifted(block[:, :HALO], "cols", -1)
        up = shifted(jnp.concatenate([left[-HALO:], block[-HALO:], right[-HALO:]], axis=1), "rows", 1)
        down = shifted(jnp.concatenate([left[:HALO], block[:HALO], right[:HALO]], axis=1), "rows", -1)
        return up, block, down, left, right
    up = shifted(block[-HALO:], "rows", 1)
    down = shifted(block[:HALO], "rows", -1)
    left = shifted(jnp.concatenate([up[:, -HALO:], block[:, -HALO:], down[:, -HALO:]], axis=0), "cols", 1)
    right = shifted(jnp.concatenate([up[:, :HALO], block[:, :HALO], down[:, :HALO]], axis=0), "cols", -1)
    return up, block, down, left, right


def all_sum(x):
    for axis in ("cols", "rows"):
        length = lax.axis_size(axis)
        if length & (length - 1):
            x = lax.psum(x, axis)
            continue
        groups, step = [], 1
        while step < length:
            radix = 4 if 4 * step <= length else 2
            groups.append((step, radix))
            step *= radix
        for step, radix in groups:
            if radix == 4:
                r1, r2, r3 = (lax.ppermute(x, axis, [(i, i ^ (k * step)) for i in range(length)]) for k in (1, 2, 3))
                x = (x + r1) + (r2 + r3)
            else:
                x = x + lax.ppermute(x, axis, [(i, i ^ step) for i in range(length)])
    return x


def summed_gram(flat):
    local = matmul(flat.T, flat)
    half = local.shape[0] // 2
    packed = all_sum(jnp.concatenate([local[:half], local[half:, half:]], axis=1))
    top = packed[:, : 2 * half]
    corner = packed[:, 2 * half :]
    bottom = jnp.concatenate([top[:, half:].T, corner], axis=1)
    return jnp.concatenate([top, bottom], axis=0)


def tv_kernel(up_ref, mid_ref, down_ref, left_ref, right_ref, kx_ref, ky_ref, fg_ref, dual_ref, cols_first=False):
    if cols_first:
        t = jnp.concatenate([left_ref[...], mid_ref[...], right_ref[...]], axis=1)
        t = jnp.concatenate([up_ref[...], t, down_ref[...]], axis=0)
    else:
        t = jnp.concatenate([up_ref[...], mid_ref[...], down_ref[...]], axis=0)
        t = jnp.concatenate([left_ref[...], t, right_ref[...]], axis=1)
    rows, cols = t.shape[0], t.shape[1]
    kx = kx_ref[...]
    ky = ky_ref[...][None]

    def prev_y(q):
        return pltpu.roll(q, 1, 1)

    def next_y(q):
        return pltpu.roll(q, cols - 1, 1)

    s = t
    px = jnp.clip(dual_step * (s[1:] - s[:-1]), -tv_weight, tv_weight) * kx[: rows - 1]
    py = jnp.clip(dual_step * (next_y(s[: rows - 1]) - s[: rows - 1]), -tv_weight, tv_weight) * ky
    for sweep in range(2, K_TV + 1):
        n = rows + 3 - 2 * sweep
        q = py[1:n]
        s = t[sweep - 1 : rows + 1 - sweep] - (px[: n - 1] - px[1:n] + prev_y(q) - q)
        down = s[1:] - s[:-1]
        across = next_y(s[:-1]) - s[:-1]
        px = jnp.clip(px[1 : n - 1] + dual_step * down, -tv_weight, tv_weight) * kx[sweep - 1 : rows - sweep]
        py = jnp.clip(py[1 : n - 1] + dual_step * across, -tv_weight, tv_weight) * ky
    q = py[1:]
    inner = rows - 2 * HALO
    middle = t[HALO : HALO + inner]
    fg = middle - (px[:-1] - px[1:] + prev_y(q) - q)
    width = cols - 2 * HALO
    fg = fg[:, HALO : HALO + width]
    fg_ref[...] = fg
    dual_ref[...] = middle[:, HALO : HALO + width] - fg


def tv_local(pieces, kx, ky, chunk, frames, into=None):
    up, mid, down, left, right = pieces
    inner_rows, inner_cols, lanes = mid.shape
    rows, cols = inner_rows + 2 * HALO, inner_cols + 2 * HALO
    out = jax.ShapeDtypeStruct((inner_rows, inner_cols, frames), jnp.float32)

    def whole(shape):
        return pl.BlockSpec(shape, lambda f: (0,) * len(shape))

    in_specs = [whole(up.shape), whole(mid.shape), whole(down.shape), whole(left.shape), whole(right.shape)]
    in_specs += [whole((rows, 1, lanes)), whole((cols, lanes))]
    operands = [up, mid, down, left, right, kx, ky]
    aliases = {}
    body = tv_kernel
    if into is not None:
        in_specs += [pl.BlockSpec(memory_space=pl.ANY), pl.BlockSpec(memory_space=pl.ANY)]
        operands += list(into)
        aliases = {7: 0, 8: 1}

        def body(*refs):
            tv_kernel(*refs[:7], *refs[9:], cols_first=True)

    return pl.pallas_call(
        body,
        grid=(1,),
        in_specs=in_specs,
        out_specs=[
            pl.BlockSpec((inner_rows, inner_cols, lanes), lambda f: (0, 0, chunk)),
            pl.BlockSpec((inner_rows, inner_cols, lanes), lambda f: (0, 0, chunk)),
        ],
        out_shape=[out, out],
        input_output_aliases=aliases,
    )(*operands)


def per_device(video, foreground, scaled_dual):
    rows_here, cols_here, frames = foreground.shape
    total_rows = rows_here * lax.axis_size("rows")
    total_cols = cols_here * lax.axis_size("cols")
    observed = video.astype(jnp.float32)
    mixed = observed - foreground + scaled_dual
    flat = mixed.reshape(-1, frames)
    gram = summed_gram(flat)
    shrink = shrink_matrix(gram)
    background = matmul(flat, shrink).reshape(foreground.shape)
    target = observed - background + scaled_dual
    ext_rows, ext_cols = rows_here + 2 * HALO, cols_here + 2 * HALO

    first_row = lax.axis_index("rows") * rows_here - HALO
    first_col = lax.axis_index("cols") * cols_here - HALO
    g = first_row + lax.broadcasted_iota(jnp.int32, (ext_rows, 1, 1), 0)
    h = first_col + lax.broadcasted_iota(jnp.int32, (1, ext_cols, 1), 1)
    lanes = 128 if frames % 128 == 0 else frames
    keep_x = (g >= 0) & (g <= total_rows - 2)
    keep_y = (h >= 0) & (h <= total_cols - 2)
    kx = jnp.broadcast_to(jnp.where(keep_x, 1.0, 0.0).astype(jnp.float32), (ext_rows, 1, lanes))
    ky = jnp.broadcast_to(jnp.where(keep_y, 1.0, 0.0).astype(jnp.float32)[0], (ext_cols, lanes))
    outs = None
    for chunk in range(frames // lanes):
        pieces = halo_pieces(target[:, :, chunk * lanes : (chunk + 1) * lanes], cols_first=chunk > 0)
        outs = tv_local(pieces, kx, ky, chunk, frames, outs)
    new_foreground, new_dual = outs
    return (background, new_foreground, new_dual)


def solution(mesh):
    return jax.shard_map(
        per_device,
        mesh=mesh,
        in_specs=(P("rows", "cols", None), P("rows", "cols", None), P("rows", "cols", None)),
        out_specs=(P("rows", "cols", None), P("rows", "cols", None), P("rows", "cols", None)),
        check_vma=False,
    )
```

```python
import jax
import jax.numpy as jnp
from jax import lax
from jax.sharding import PartitionSpec as P
from jax.experimental import pallas as pl
from jax.experimental.pallas import tpu as pltpu


K_ROOT = 8
K_SIGN = 6
K_TV = 8


threshold_ratio = 1.0
dual_step = 0.25
tv_weight = 1.0

HALO = K_TV


def shifted(x, axis, by):
    length = lax.axis_size(axis)
    pairs = [(i, i + by) for i in range(length) if 0 <= i + by < length]
    return lax.ppermute(x, axis, pairs)


def matmul(left, right):
    return jnp.dot(left, right, precision=lax.Precision.HIGH, preferred_element_type=jnp.float32)


def shrink_matrix(gram):
    size = gram.shape[0]
    identity = jnp.eye(size, dtype=jnp.float32)
    scale = jnp.sqrt(jnp.sum(gram * gram))
    root = gram / scale
    inverse = identity
    for _ in range(K_ROOT):
        factor = 1.5 * identity - 0.5 * matmul(inverse, root)
        root = matmul(root, factor)
        inverse = matmul(factor, inverse)
    cutoff = threshold_ratio * jnp.trace(root) / size
    signed = root - cutoff * identity
    for _ in range(K_SIGN):
        signed = 1.5 * signed - 0.5 * matmul(signed, matmul(signed, signed))
    return 0.5 * matmul(identity - cutoff * inverse, identity + signed)


def halo_pieces(block, cols_first=False):
    if cols_first:
        left = shifted(block[:, -HALO:], "cols", 1)
        right = shifted(block[:, :HALO], "cols", -1)
        up = shifted(jnp.concatenate([left[-HALO:], block[-HALO:], right[-HALO:]], axis=1), "rows", 1)
        down = shifted(jnp.concatenate([left[:HALO], block[:HALO], right[:HALO]], axis=1), "rows", -1)
        return up, block, down, left, right
    up = shifted(block[-HALO:], "rows", 1)
    down = shifted(block[:HALO], "rows", -1)
    left = shifted(jnp.concatenate([up[:, -HALO:], block[:, -HALO:], down[:, -HALO:]], axis=0), "cols", 1)
    right = shifted(jnp.concatenate([up[:, :HALO], block[:, :HALO], down[:, :HALO]], axis=0), "cols", -1)
    return up, block, down, left, right


def all_sum(x):
    for axis in ("cols", "rows"):
        length = lax.axis_size(axis)
        if length & (length - 1):
            x = lax.psum(x, axis)
            continue
        groups, step = [], 1
        while step < length:
            radix = 4 if 4 * step <= length else 2
            groups.append((step, radix))
            step *= radix
        for step, radix in groups:
            if radix == 4:
                r1, r2, r3 = (lax.ppermute(x, axis, [(i, i ^ (k * step)) for i in range(length)]) for k in (1, 2, 3))
                x = (x + r1) + (r2 + r3)
            else:
                x = x + lax.ppermute(x, axis, [(i, i ^ step) for i in range(length)])
    return x


def summed_gram(flat):
    local = matmul(flat.T, flat)
    size = local.shape[0]
    block = 32 if size % 32 == 0 else size
    n = size // block
    upper = [(i, j) for i in range(n) for j in range(i, n)]
    packed = jnp.concatenate([local[i * block : (i + 1) * block, j * block : (j + 1) * block] for i, j in upper], axis=1)
    packed = all_sum(packed)
    piece = {ij: packed[:, k * block : (k + 1) * block] for k, ij in enumerate(upper)}
    rows = [jnp.concatenate([piece[(i, j)] if i <= j else piece[(j, i)].T for j in range(n)], axis=1) for i in range(n)]
    return jnp.concatenate(rows, axis=0)


def tv_kernel(up_ref, mid_ref, down_ref, left_ref, right_ref, kx_ref, ky_ref, fg_ref, dual_ref, cols_first=False):
    if cols_first:
        t = jnp.concatenate([left_ref[...], mid_ref[...], right_ref[...]], axis=1)
        t = jnp.concatenate([up_ref[...], t, down_ref[...]], axis=0)
    else:
        t = jnp.concatenate([up_ref[...], mid_ref[...], down_ref[...]], axis=0)
        t = jnp.concatenate([left_ref[...], t, right_ref[...]], axis=1)
    rows, cols = t.shape[0], t.shape[1]
    kx = kx_ref[...]
    ky = ky_ref[...][None]

    def prev_y(q):
        return pltpu.roll(q, 1, 1)

    def next_y(q):
        return pltpu.roll(q, cols - 1, 1)

    s = t
    px = jnp.clip(dual_step * (s[1:] - s[:-1]), -tv_weight, tv_weight) * kx[: rows - 1]
    py = jnp.clip(dual_step * (next_y(s[: rows - 1]) - s[: rows - 1]), -tv_weight, tv_weight) * ky
    for sweep in range(2, K_TV + 1):
        n = rows + 3 - 2 * sweep
        q = py[1:n]
        s = t[sweep - 1 : rows + 1 - sweep] - (px[: n - 1] - px[1:n] + prev_y(q) - q)
        down = s[1:] - s[:-1]
        across = next_y(s[:-1]) - s[:-1]
        px = jnp.clip(px[1 : n - 1] + dual_step * down, -tv_weight, tv_weight) * kx[sweep - 1 : rows - sweep]
        py = jnp.clip(py[1 : n - 1] + dual_step * across, -tv_weight, tv_weight) * ky
    q = py[1:]
    inner = rows - 2 * HALO
    middle = t[HALO : HALO + inner]
    fg = middle - (px[:-1] - px[1:] + prev_y(q) - q)
    width = cols - 2 * HALO
    fg = fg[:, HALO : HALO + width]
    fg_ref[...] = fg
    dual_ref[...] = middle[:, HALO : HALO + width] - fg


def tv_local(pieces, kx, ky, chunk, frames, into=None):
    up, mid, down, left, right = pieces
    inner_rows, inner_cols, lanes = mid.shape
    rows, cols = inner_rows + 2 * HALO, inner_cols + 2 * HALO
    out = jax.ShapeDtypeStruct((inner_rows, inner_cols, frames), jnp.float32)

    def whole(shape):
        return pl.BlockSpec(shape, lambda f: (0,) * len(shape))

    in_specs = [whole(up.shape), whole(mid.shape), whole(down.shape), whole(left.shape), whole(right.shape)]
    in_specs += [whole((rows, 1, lanes)), whole((cols, lanes))]
    operands = [up, mid, down, left, right, kx, ky]
    aliases = {}
    body = tv_kernel
    if into is not None:
        in_specs += [pl.BlockSpec(memory_space=pl.ANY), pl.BlockSpec(memory_space=pl.ANY)]
        operands += list(into)
        aliases = {7: 0, 8: 1}

        def body(*refs):
            tv_kernel(*refs[:7], *refs[9:], cols_first=True)

    return pl.pallas_call(
        body,
        grid=(1,),
        in_specs=in_specs,
        out_specs=[
            pl.BlockSpec((inner_rows, inner_cols, lanes), lambda f: (0, 0, chunk)),
            pl.BlockSpec((inner_rows, inner_cols, lanes), lambda f: (0, 0, chunk)),
        ],
        out_shape=[out, out],
        input_output_aliases=aliases,
    )(*operands)


def per_device(video, foreground, scaled_dual):
    rows_here, cols_here, frames = foreground.shape
    total_rows = rows_here * lax.axis_size("rows")
    total_cols = cols_here * lax.axis_size("cols")
    observed = video.astype(jnp.float32)
    mixed = observed - foreground + scaled_dual
    flat = mixed.reshape(-1, frames)
    gram = summed_gram(flat)
    shrink = shrink_matrix(gram)
    background = matmul(flat, shrink).reshape(foreground.shape)
    target = observed - background + scaled_dual
    ext_rows, ext_cols = rows_here + 2 * HALO, cols_here + 2 * HALO

    first_row = lax.axis_index("rows") * rows_here - HALO
    first_col = lax.axis_index("cols") * cols_here - HALO
    g = first_row + lax.broadcasted_iota(jnp.int32, (ext_rows, 1, 1), 0)
    h = first_col + lax.broadcasted_iota(jnp.int32, (1, ext_cols, 1), 1)
    lanes = 128 if frames % 128 == 0 else frames
    keep_x = (g >= 0) & (g <= total_rows - 2)
    keep_y = (h >= 0) & (h <= total_cols - 2)
    kx = jnp.broadcast_to(jnp.where(keep_x, 1.0, 0.0).astype(jnp.float32), (ext_rows, 1, lanes))
    ky = jnp.broadcast_to(jnp.where(keep_y, 1.0, 0.0).astype(jnp.float32)[0], (ext_cols, lanes))
    outs = None
    for chunk in range(frames // lanes):
        pieces = halo_pieces(target[:, :, chunk * lanes : (chunk + 1) * lanes], cols_first=chunk > 0)
        outs = tv_local(pieces, kx, ky, chunk, frames, outs)
    new_foreground, new_dual = outs
    return (background, new_foreground, new_dual)


def solution(mesh):
    return jax.shard_map(
        per_device,
        mesh=mesh,
        in_specs=(P("rows", "cols", None), P("rows", "cols", None), P("rows", "cols", None)),
        out_specs=(P("rows", "cols", None), P("rows", "cols", None), P("rows", "cols", None)),
        check_vma=False,
    )
```

```python
import jax
import jax.numpy as jnp
from jax import lax
from jax.sharding import PartitionSpec as P
from jax.experimental import pallas as pl
from jax.experimental.pallas import tpu as pltpu


K_ROOT = 8
K_SIGN = 6
K_TV = 8


threshold_ratio = 1.0
dual_step = 0.25
tv_weight = 1.0

HALO = K_TV


def shifted(x, axis, by):
    length = lax.axis_size(axis)
    pairs = [(i, i + by) for i in range(length) if 0 <= i + by < length]
    return lax.ppermute(x, axis, pairs)


def matmul(left, right):
    return jnp.dot(left, right, precision=lax.Precision.HIGH, preferred_element_type=jnp.float32)


def shrink_matrix(gram):
    size = gram.shape[0]
    identity = jnp.eye(size, dtype=jnp.float32)
    scale = jnp.sqrt(jnp.sum(gram * gram))
    root = gram / scale
    inverse = identity
    for _ in range(K_ROOT):
        factor = 1.5 * identity - 0.5 * matmul(inverse, root)
        root = matmul(root, factor)
        inverse = matmul(factor, inverse)
    cutoff = threshold_ratio * jnp.trace(root) / size
    signed = root - cutoff * identity
    for _ in range(K_SIGN):
        signed = 1.5 * signed - 0.5 * matmul(signed, matmul(signed, signed))
    return 0.5 * matmul(identity - cutoff * inverse, identity + signed)


def halo_pieces(block, cols_first=False):
    if cols_first:
        left = shifted(block[:, -HALO:], "cols", 1)
        right = shifted(block[:, :HALO], "cols", -1)
        up = shifted(jnp.concatenate([left[-HALO:], block[-HALO:], right[-HALO:]], axis=1), "rows", 1)
        down = shifted(jnp.concatenate([left[:HALO], block[:HALO], right[:HALO]], axis=1), "rows", -1)
        return up, block, down, left, right
    up = shifted(block[-HALO:], "rows", 1)
    down = shifted(block[:HALO], "rows", -1)
    left = shifted(jnp.concatenate([up[:, -HALO:], block[:, -HALO:], down[:, -HALO:]], axis=0), "cols", 1)
    right = shifted(jnp.concatenate([up[:, :HALO], block[:, :HALO], down[:, :HALO]], axis=0), "cols", -1)
    return up, block, down, left, right


def all_sum(x):
    for axis in ("cols", "rows"):
        length = lax.axis_size(axis)
        if length & (length - 1):
            x = lax.psum(x, axis)
            continue
        groups, step = [], 1
        while step < length:
            radix = 4 if 4 * step <= length else 2
            groups.append((step, radix))
            step *= radix
        for step, radix in groups:
            if radix == 4:
                r1, r2, r3 = (lax.ppermute(x, axis, [(i, i ^ (k * step)) for i in range(length)]) for k in (1, 2, 3))
                x = (x + r1) + (r2 + r3)
            else:
                x = x + lax.ppermute(x, axis, [(i, i ^ step) for i in range(length)])
    return x


def summed_gram(flat):
    local = matmul(flat.T, flat)
    size = local.shape[0]
    block = 32
    n = size // block
    if size % block or n % 2:
        return all_sum(local)
    packed = jnp.concatenate(
        [
            jnp.concatenate([local[k * block : (k + 1) * block, k * block :], local[size - (k + 1) * block : size - k * block, size - (k + 1) * block :]], axis=1)
            for k in range(n // 2)
        ],
        axis=0,
    )
    packed = all_sum(packed.T).T
    rows = [None] * n
    for k in range(n // 2):
        pair = packed[k * block : (k + 1) * block]
        rows[k] = pair[:, : (n - k) * block]
        rows[n - 1 - k] = pair[:, (n - k) * block :]
    upper = jnp.concatenate([jnp.pad(r, ((0, 0), (size - r.shape[1], 0))) for r in rows], axis=0)
    block_row = lax.broadcasted_iota(jnp.int32, (size, size), 0) // block
    block_col = lax.broadcasted_iota(jnp.int32, (size, size), 1) // block
    return jnp.where(block_row <= block_col, upper, upper.T)


def tv_kernel(up_ref, mid_ref, down_ref, left_ref, right_ref, kx_ref, ky_ref, fg_ref, dual_ref, cols_first=False):
    if cols_first:
        t = jnp.concatenate([left_ref[...], mid_ref[...], right_ref[...]], axis=1)
        t = jnp.concatenate([up_ref[...], t, down_ref[...]], axis=0)
    else:
        t = jnp.concatenate([up_ref[...], mid_ref[...], down_ref[...]], axis=0)
        t = jnp.concatenate([left_ref[...], t, right_ref[...]], axis=1)
    rows, cols = t.shape[0], t.shape[1]
    kx = kx_ref[...]
    ky = ky_ref[...][None]

    def prev_y(q):
        return pltpu.roll(q, 1, 1)

    def next_y(q):
        return pltpu.roll(q, cols - 1, 1)

    s = t
    px = jnp.clip(dual_step * (s[1:] - s[:-1]), -tv_weight, tv_weight) * kx[: rows - 1]
    py = jnp.clip(dual_step * (next_y(s[: rows - 1]) - s[: rows - 1]), -tv_weight, tv_weight) * ky
    for sweep in range(2, K_TV + 1):
        n = rows + 3 - 2 * sweep
        q = py[1:n]
        s = t[sweep - 1 : rows + 1 - sweep] - (px[: n - 1] - px[1:n] + prev_y(q) - q)
        down = s[1:] - s[:-1]
        across = next_y(s[:-1]) - s[:-1]
        px = jnp.clip(px[1 : n - 1] + dual_step * down, -tv_weight, tv_weight) * kx[sweep - 1 : rows - sweep]
        py = jnp.clip(py[1 : n - 1] + dual_step * across, -tv_weight, tv_weight) * ky
    q = py[1:]
    inner = rows - 2 * HALO
    middle = t[HALO : HALO + inner]
    fg = middle - (px[:-1] - px[1:] + prev_y(q) - q)
    width = cols - 2 * HALO
    fg = fg[:, HALO : HALO + width]
    fg_ref[...] = fg
    dual_ref[...] = middle[:, HALO : HALO + width] - fg


def tv_local(pieces, kx, ky, chunk, frames, into=None):
    up, mid, down, left, right = pieces
    inner_rows, inner_cols, lanes = mid.shape
    rows, cols = inner_rows + 2 * HALO, inner_cols + 2 * HALO
    out = jax.ShapeDtypeStruct((inner_rows, inner_cols, frames), jnp.float32)

    def whole(shape):
        return pl.BlockSpec(shape, lambda f: (0,) * len(shape))

    in_specs = [whole(up.shape), whole(mid.shape), whole(down.shape), whole(left.shape), whole(right.shape)]
    in_specs += [whole((rows, 1, lanes)), whole((cols, lanes))]
    operands = [up, mid, down, left, right, kx, ky]
    aliases = {}
    body = tv_kernel
    if into is not None:
        in_specs += [pl.BlockSpec(memory_space=pl.ANY), pl.BlockSpec(memory_space=pl.ANY)]
        operands += list(into)
        aliases = {7: 0, 8: 1}

        def body(*refs):
            tv_kernel(*refs[:7], *refs[9:], cols_first=True)

    return pl.pallas_call(
        body,
        grid=(1,),
        in_specs=in_specs,
        out_specs=[
            pl.BlockSpec((inner_rows, inner_cols, lanes), lambda f: (0, 0, chunk)),
            pl.BlockSpec((inner_rows, inner_cols, lanes), lambda f: (0, 0, chunk)),
        ],
        out_shape=[out, out],
        input_output_aliases=aliases,
    )(*operands)


def per_device(video, foreground, scaled_dual):
    rows_here, cols_here, frames = foreground.shape
    total_rows = rows_here * lax.axis_size("rows")
    total_cols = cols_here * lax.axis_size("cols")
    observed = video.astype(jnp.float32)
    mixed = observed - foreground + scaled_dual
    flat = mixed.reshape(-1, frames)
    gram = summed_gram(flat)
    shrink = shrink_matrix(gram)
    background = matmul(flat, shrink).reshape(foreground.shape)
    target = observed - background + scaled_dual
    ext_rows, ext_cols = rows_here + 2 * HALO, cols_here + 2 * HALO

    first_row = lax.axis_index("rows") * rows_here - HALO
    first_col = lax.axis_index("cols") * cols_here - HALO
    g = first_row + lax.broadcasted_iota(jnp.int32, (ext_rows, 1, 1), 0)
    h = first_col + lax.broadcasted_iota(jnp.int32, (1, ext_cols, 1), 1)
    lanes = 128 if frames % 128 == 0 else frames
    keep_x = (g >= 0) & (g <= total_rows - 2)
    keep_y = (h >= 0) & (h <= total_cols - 2)
    kx = jnp.broadcast_to(jnp.where(keep_x, 1.0, 0.0).astype(jnp.float32), (ext_rows, 1, lanes))
    ky = jnp.broadcast_to(jnp.where(keep_y, 1.0, 0.0).astype(jnp.float32)[0], (ext_cols, lanes))
    outs = None
    for chunk in range(frames // lanes):
        pieces = halo_pieces(target[:, :, chunk * lanes : (chunk + 1) * lanes], cols_first=chunk > 0)
        outs = tv_local(pieces, kx, ky, chunk, frames, outs)
    new_foreground, new_dual = outs
    return (background, new_foreground, new_dual)


def solution(mesh):
    return jax.shard_map(
        per_device,
        mesh=mesh,
        in_specs=(P("rows", "cols", None), P("rows", "cols", None), P("rows", "cols", None)),
        out_specs=(P("rows", "cols", None), P("rows", "cols", None), P("rows", "cols", None)),
        check_vma=False,
    )
```

```python
import jax
import jax.numpy as jnp
from jax import lax
from jax.sharding import PartitionSpec as P
from jax.experimental import pallas as pl
from jax.experimental.pallas import tpu as pltpu


K_ROOT = 8
K_SIGN = 6
K_TV = 8


threshold_ratio = 1.0
dual_step = 0.25
tv_weight = 1.0

HALO = K_TV


def shifted(x, axis, by):
    length = lax.axis_size(axis)
    pairs = [(i, i + by) for i in range(length) if 0 <= i + by < length]
    return lax.ppermute(x, axis, pairs)


def matmul(left, right):
    return jnp.dot(left, right, precision=lax.Precision.HIGH, preferred_element_type=jnp.float32)


def shrink_matrix(gram):
    size = gram.shape[0]
    identity = jnp.eye(size, dtype=jnp.float32)
    scale = jnp.sqrt(jnp.sum(gram * gram))
    root = gram / scale
    inverse = identity
    for _ in range(K_ROOT):
        factor = 1.5 * identity - 0.5 * matmul(inverse, root)
        root = matmul(root, factor)
        inverse = matmul(factor, inverse)
    cutoff = threshold_ratio * jnp.trace(root) / size
    signed = root - cutoff * identity
    for _ in range(K_SIGN):
        signed = 1.5 * signed - 0.5 * matmul(signed, matmul(signed, signed))
    return 0.5 * matmul(identity - cutoff * inverse, identity + signed)


def halo_pieces(block, cols_first=False):
    if cols_first:
        left = shifted(block[:, -HALO:], "cols", 1)
        right = shifted(block[:, :HALO], "cols", -1)
        up = shifted(jnp.concatenate([left[-HALO:], block[-HALO:], right[-HALO:]], axis=1), "rows", 1)
        down = shifted(jnp.concatenate([left[:HALO], block[:HALO], right[:HALO]], axis=1), "rows", -1)
        return up, block, down, left, right
    up = shifted(block[-HALO:], "rows", 1)
    down = shifted(block[:HALO], "rows", -1)
    left = shifted(jnp.concatenate([up[:, -HALO:], block[:, -HALO:], down[:, -HALO:]], axis=0), "cols", 1)
    right = shifted(jnp.concatenate([up[:, :HALO], block[:, :HALO], down[:, :HALO]], axis=0), "cols", -1)
    return up, block, down, left, right


def all_sum(x):
    for axis in ("cols", "rows"):
        length = lax.axis_size(axis)
        if length & (length - 1):
            x = lax.psum(x, axis)
            continue
        groups, step = [], 1
        while step < length:
            radix = 4 if 4 * step <= length else 2
            groups.append((step, radix))
            step *= radix
        for step, radix in groups:
            if radix == 4:
                r1, r2, r3 = (lax.ppermute(x, axis, [(i, i ^ (k * step)) for i in range(length)]) for k in (1, 2, 3))
                x = (x + r1) + (r2 + r3)
            else:
                x = x + lax.ppermute(x, axis, [(i, i ^ step) for i in range(length)])
    return x


def summed_gram(flat):
    local = matmul(flat.T, flat)
    size = local.shape[0]
    block = 32 if size % 32 == 0 else size
    n = size // block
    upper = [(i, j) for i in range(n) for j in range(i, n)]
    packed = jnp.concatenate([local[i * block : (i + 1) * block, j * block : (j + 1) * block] for i, j in upper], axis=1)
    packed = all_sum(packed)
    rows, start = [], 0
    for i in range(n):
        width = (n - i) * block
        rows.append(jnp.pad(packed[:, start : start + width], ((0, 0), (size - width, 0))))
        start += width
    upper_part = jnp.concatenate(rows, axis=0)
    block_row = lax.broadcasted_iota(jnp.int32, (size, size), 0) // block
    block_col = lax.broadcasted_iota(jnp.int32, (size, size), 1) // block
    return jnp.where(block_row <= block_col, upper_part, upper_part.T)


def tv_kernel(up_ref, mid_ref, down_ref, left_ref, right_ref, kx_ref, ky_ref, fg_ref, dual_ref, cols_first=False):
    if cols_first:
        t = jnp.concatenate([left_ref[...], mid_ref[...], right_ref[...]], axis=1)
        t = jnp.concatenate([up_ref[...], t, down_ref[...]], axis=0)
    else:
        t = jnp.concatenate([up_ref[...], mid_ref[...], down_ref[...]], axis=0)
        t = jnp.concatenate([left_ref[...], t, right_ref[...]], axis=1)
    rows, cols = t.shape[0], t.shape[1]
    kx = kx_ref[...]
    ky = ky_ref[...][None]

    def prev_y(q):
        return pltpu.roll(q, 1, 1)

    def next_y(q):
        return pltpu.roll(q, cols - 1, 1)

    s = t
    px = jnp.clip(dual_step * (s[1:] - s[:-1]), -tv_weight, tv_weight) * kx[: rows - 1]
    py = jnp.clip(dual_step * (next_y(s[: rows - 1]) - s[: rows - 1]), -tv_weight, tv_weight) * ky
    for sweep in range(2, K_TV + 1):
        n = rows + 3 - 2 * sweep
        q = py[1:n]
        s = t[sweep - 1 : rows + 1 - sweep] - (px[: n - 1] - px[1:n] + prev_y(q) - q)
        down = s[1:] - s[:-1]
        across = next_y(s[:-1]) - s[:-1]
        px = jnp.clip(px[1 : n - 1] + dual_step * down, -tv_weight, tv_weight) * kx[sweep - 1 : rows - sweep]
        py = jnp.clip(py[1 : n - 1] + dual_step * across, -tv_weight, tv_weight) * ky
    q = py[1:]
    inner = rows - 2 * HALO
    middle = t[HALO : HALO + inner]
    fg = middle - (px[:-1] - px[1:] + prev_y(q) - q)
    width = cols - 2 * HALO
    fg = fg[:, HALO : HALO + width]
    fg_ref[...] = fg
    dual_ref[...] = middle[:, HALO : HALO + width] - fg


def tv_local(pieces, kx, ky, chunk, frames, into=None):
    up, mid, down, left, right = pieces
    inner_rows, inner_cols, lanes = mid.shape
    rows, cols = inner_rows + 2 * HALO, inner_cols + 2 * HALO
    out = jax.ShapeDtypeStruct((inner_rows, inner_cols, frames), jnp.float32)

    def whole(shape):
        return pl.BlockSpec(shape, lambda f: (0,) * len(shape))

    in_specs = [whole(up.shape), whole(mid.shape), whole(down.shape), whole(left.shape), whole(right.shape)]
    in_specs += [whole((rows, 1, lanes)), whole((cols, lanes))]
    operands = [up, mid, down, left, right, kx, ky]
    aliases = {}
    body = tv_kernel
    if into is not None:
        in_specs += [pl.BlockSpec(memory_space=pl.ANY), pl.BlockSpec(memory_space=pl.ANY)]
        operands += list(into)
        aliases = {7: 0, 8: 1}

        def body(*refs):
            tv_kernel(*refs[:7], *refs[9:], cols_first=True)

    return pl.pallas_call(
        body,
        grid=(1,),
        in_specs=in_specs,
        out_specs=[
            pl.BlockSpec((inner_rows, inner_cols, lanes), lambda f: (0, 0, chunk)),
            pl.BlockSpec((inner_rows, inner_cols, lanes), lambda f: (0, 0, chunk)),
        ],
        out_shape=[out, out],
        input_output_aliases=aliases,
    )(*operands)


def per_device(video, foreground, scaled_dual):
    rows_here, cols_here, frames = foreground.shape
    total_rows = rows_here * lax.axis_size("rows")
    total_cols = cols_here * lax.axis_size("cols")
    observed = video.astype(jnp.float32)
    mixed = observed - foreground + scaled_dual
    flat = mixed.reshape(-1, frames)
    gram = summed_gram(flat)
    shrink = shrink_matrix(gram)
    background = matmul(flat, shrink).reshape(foreground.shape)
    target = observed - background + scaled_dual
    ext_rows, ext_cols = rows_here + 2 * HALO, cols_here + 2 * HALO

    first_row = lax.axis_index("rows") * rows_here - HALO
    first_col = lax.axis_index("cols") * cols_here - HALO
    g = first_row + lax.broadcasted_iota(jnp.int32, (ext_rows, 1, 1), 0)
    h = first_col + lax.broadcasted_iota(jnp.int32, (1, ext_cols, 1), 1)
    lanes = 128 if frames % 128 == 0 else frames
    keep_x = (g >= 0) & (g <= total_rows - 2)
    keep_y = (h >= 0) & (h <= total_cols - 2)
    kx = jnp.broadcast_to(jnp.where(keep_x, 1.0, 0.0).astype(jnp.float32), (ext_rows, 1, lanes))
    ky = jnp.broadcast_to(jnp.where(keep_y, 1.0, 0.0).astype(jnp.float32)[0], (ext_cols, lanes))
    outs = None
    for chunk in range(frames // lanes):
        pieces = halo_pieces(target[:, :, chunk * lanes : (chunk + 1) * lanes], cols_first=chunk > 0)
        outs = tv_local(pieces, kx, ky, chunk, frames, outs)
    new_foreground, new_dual = outs
    return (background, new_foreground, new_dual)


def solution(mesh):
    return jax.shard_map(
        per_device,
        mesh=mesh,
        in_specs=(P("rows", "cols", None), P("rows", "cols", None), P("rows", "cols", None)),
        out_specs=(P("rows", "cols", None), P("rows", "cols", None), P("rows", "cols", None)),
        check_vma=False,
    )
```
